512 devices in a mesh: seq: 128 (over y, z, core), mp: 4 (over x).
Axes of the slice: x: 4, y: 8, z: 8, core: 2. Of those that a mesh axis runs over, the one named last changes fastest.
Arguments:
- fresh_queries: bfloat16 [8192, 2048], P('seq', 'mp'), may hold values from -120 to 120
- fresh_keys: bfloat16 [8192, 1024], P('seq', 'mp'), may hold values from -6 to 6
- fresh_values: bfloat16 [8192, 1024], P('seq', 'mp'), may hold values from -6 to 6
- cache: bfloat16 [2, 8192, 1024], P(None, 'seq', 'mp'), may hold values from -6 to 6
- pool_root: int32 [128, 32], replicated, may hold values from 0 to 31
- branch_owner: int32 [128], replicated, may hold values from 0 to 127, each once
- branch_len: int32 [128], replicated, may hold values from 1 to 32, 2048 in all
- branch_root: int32 [128], replicated, may hold values from 0 to 31
- request_branch: int32 [128, 4], P('seq'), may hold values from 0 to 127
- token_request: int32 [128, 64], P('seq'), may hold values from 0 to 3, never falling along the last dimension, each value on 1 to 32 neighbouring positions
- residual: bfloat16 [8192, 2048], P('seq'), may hold values from -1.5 to 1.5
- wo_t: bfloat16 [2048, 2048], P('seq', 'mp'), may hold values from -0.125 to 0.125
- norm_gain: float32 [2048], replicated, may hold values from 0.1 to 1.9
- w_qkv: bfloat16 [2048, 4096], P('seq', 'mp'), may hold values from -0.125 to 0.125
Outputs:
- attn: bfloat16 [8192, 2048], P('seq', 'mp')
- stream: bfloat16 [8192, 2048], P('seq')
- qkv_next: bfloat16 [8192, 4096], P('seq', 'mp')
The draws below stay inside these ranges and needn't reach their ends.
Inputs may be any that keep to these rules, and one draw needn't show every extreme that they name: `token_request`: in each index's row the request number never falls, and each request has 1 to 32 tokens. `branch_owner`: each index of seq holds exactly one branch. `branch_len`: the longest branch has 32 rows.
All inputs are finite; a program needn't handle non-finite values.
Results may differ from the reference program's by a relative error of at most 0.018.
Values may be sent and summed in bfloat16 or wider, within the bound.
A program may use at most 64 MiB of HBM per device.

```python
import math
import jax
import jax.numpy as jnp
import numpy as np
from jax import lax

D = 2048
QUERY_HEADS = 16
KEY_VALUE_HEADS = 8
HEAD_SIZE = 128
TOKENS_PER_SEQ = 64
REQ_DEV = 4
ROOT_DEV = 32
BRANCH_CAP = 32
NEW_TOKENS = 8192
BRANCHES = 128
ROOTS = 32
CACHED_ROWS = 8192
QKVW = 4096
N_SEQ = 128


def drawn_draws(key):
    base_offset = jnp.clip(jax.random.normal(jax.random.fold_in(key, 101), (NEW_TOKENS, KEY_VALUE_HEADS, HEAD_SIZE), jnp.float32), -6.0, 6.0)
    drawn = jnp.clip(jax.random.normal(jax.random.fold_in(key, 102), (NEW_TOKENS, QUERY_HEADS * HEAD_SIZE), jnp.float32), -6.0, 6.0)
    query_rows = drawn
    key_row_block = base_offset.reshape(NEW_TOKENS, KEY_VALUE_HEADS * HEAD_SIZE)
    return (query_rows, key_row_block)


def draw_fresh_queries(key, part):
    query_rows, key_row_block = drawn_draws(key)
    return query_rows.astype(jnp.bfloat16)


def draw_fresh_keys(key, part):
    query_rows, key_row_block = drawn_draws(key)
    return key_row_block.astype(jnp.bfloat16)


def place_ends(values, key, low, largest):
    spot = [jax.random.randint(jax.random.fold_in(key, axis), (), 0, length) for axis, length in enumerate(values.shape)]
    widest = values.shape.index(max(values.shape))
    neighbour = spot[:widest] + [(spot[widest] + 1) % values.shape[widest]] + spot[widest + 1:]
    return values.at[tuple(spot)].set(low).at[tuple(neighbour)].set(largest)


def levels(key, extent, split, low, largest):
    gain = 1.0
    for dim, blocks in split:
        heights = jax.random.uniform(jax.random.fold_in(jax.random.fold_in(key, 6), dim), (blocks,), jnp.float32, low / len(split), largest / len(split))
        gain = gain * jnp.repeat(jnp.exp(heights), extent[dim] // blocks).reshape((-1,) + (1,) * (len(extent) - 1 - dim))
    return gain


def cumulative_ranks(amount, slope):
    portions = [(1 << 20) // math.isqrt(grade ** slope) + 1 for grade in range(1, amount + 1)]
    deviation = 1 + sum(portions) // (1 << 30)
    return np.cumsum(np.array([max(1, weight // deviation) for weight in portions]))


def ranked_ids(rng, shape, amount, skew):
    listing = cumulative_ranks(amount, skew)
    ticket = jax.random.randint(jax.random.fold_in(rng, 1), shape, 0, int(listing[amount - 1]))
    grade = jnp.searchsorted(jnp.asarray(listing, jnp.int32), ticket, side="right")
    return jax.random.permutation(jax.random.fold_in(rng, 2), amount)[grade].astype(jnp.int32)


def profile(amount, total, most, lean):
    portions = [(1 << 20) // math.isqrt(grade ** lean) + 1 for grade in range(2, amount + 1)]
    spare, given = total - most - (amount - 1), [1] * (amount - 1)
    while spare > 0:
        movable = [i for i in range(amount - 1) if given[i] < most]
        whole, left = sum([portions[i] for i in movable]), spare
        for i in movable:
            extra = min(most - given[i], max(1, left * portions[i] // whole), spare)
            given[i] = given[i] + extra
            spare = spare - extra
    return np.array([most] + given)


def uneven(key, amount, total, bound, slope):
    if amount == 2:
        one = jax.random.randint(key, (), max(1, total - bound), min(bound, total - 1) + 1)
        return jnp.stack([one, total - one])
    lengths = jnp.asarray(profile(amount, total, bound, slope), jnp.int32)
    pairs = (amount - 1) // 2
    donor, sink = lengths[1:1 + 2 * pairs:2], lengths[2:2 + 2 * pairs:2]
    slack = jnp.minimum(donor - 1, bound - sink)
    moved = jax.random.randint(jax.random.fold_in(key, 1), (pairs,), 0, 1 << 20) % (slack + 1)
    lengths = lengths.at[1:1 + 2 * pairs:2].set(donor - moved).at[2:2 + 2 * pairs:2].set(sink + moved)
    return lengths[jax.random.permutation(jax.random.fold_in(key, 2), amount)]


def normal_values(stream_key, extent, scale, most, split=(), kind=jnp.bfloat16):
    values = jax.random.normal(stream_key, extent, jnp.float32) * scale
    if len(split) > 0:
        values = levels(stream_key, extent, split, -0.22, 0.18) * values
    return jnp.clip(values, min=-most, max=most).astype(kind)


def setup_inputs(seed: int = 0) -> dict:
    key_list = jax.random.split(jax.random.key(seed), 15)
    fresh_queries = draw_fresh_queries(jax.random.fold_in(key_list[14], 71), 0)
    fresh_keys = draw_fresh_keys(jax.random.fold_in(key_list[14], 71), 0)
    fresh_values = normal_values(key_list[2], (NEW_TOKENS, KEY_VALUE_HEADS * HEAD_SIZE), 1.0, 6.0, ((0, 128), (1, 4)))
    cache = normal_values(key_list[3], (2, CACHED_ROWS, KEY_VALUE_HEADS * HEAD_SIZE), 1.0, 6.0, ((1, 128), (2, 4)))
    pool_root = place_ends(ranked_ids(key_list[4], (N_SEQ, ROOT_DEV), ROOTS, 2), jax.random.fold_in(key_list[4], 3), 0, ROOTS - 1).astype(jnp.int32)
    branch_owner = jax.random.permutation(key_list[5], BRANCHES).astype(jnp.int32)
    branch_len = uneven(key_list[6], BRANCHES, BRANCHES * BRANCH_CAP // 2, BRANCH_CAP, 2).astype(jnp.int32)
    branch_root = place_ends(jax.random.randint(key_list[7], (BRANCHES,), 0, ROOTS), jax.random.fold_in(key_list[7], 1), 0, ROOTS - 1).astype(jnp.int32)
    request_branch = place_ends(ranked_ids(key_list[8], (N_SEQ, REQ_DEV), BRANCHES, 2), jax.random.fold_in(key_list[8], 3), 0, BRANCHES - 1).astype(jnp.int32)
    token_request = jax.vmap(lambda own: jnp.searchsorted(jnp.cumsum(uneven(own, REQ_DEV, TOKENS_PER_SEQ, TOKENS_PER_SEQ // 2, 2)), jnp.arange(TOKENS_PER_SEQ), side="right"))(jax.random.split(key_list[9], N_SEQ)).reshape((N_SEQ, TOKENS_PER_SEQ)).astype(jnp.int32)
    residual = normal_values(key_list[10], (NEW_TOKENS, D), 0.25, 1.5, ((0, 128),))
    wo_t = normal_values(key_list[11], (D, QUERY_HEADS * HEAD_SIZE), (QUERY_HEADS * HEAD_SIZE) ** -0.5, 0.125, ((0, 128), (1, 4)))
    norm_gain = jnp.clip(1.0 + 0.18 * jax.random.normal(key_list[12], (D,), jnp.float32), 0.1, 1.9)
    w_qkv = normal_values(key_list[13], (D, QKVW), D ** -0.5, 0.125, ((0, 128), (1, 4)))
    return {"fresh_queries": fresh_queries, "fresh_keys": fresh_keys, "fresh_values": fresh_values, "cache": cache, "pool_root": pool_root, "branch_owner": branch_owner, "branch_len": branch_len, "branch_root": branch_root, "request_branch": request_branch, "token_request": token_request, "residual": residual, "wo_t": wo_t, "norm_gain": norm_gain, "w_qkv": w_qkv}


def cache_tags(pool_root, branch_owner, branch_len, root_count, slot_count):
    owner_count = pool_root.shape[0]
    branch_count = branch_owner.shape[0]
    branch_ids = jnp.arange(branch_count, dtype=jnp.int32)
    owner_ids = jnp.arange(owner_count, dtype=jnp.int32)
    owned = lax.optimization_barrier(jnp.sum(jnp.where(branch_owner[None, :] == owner_ids[:, None], branch_ids[None, :], 0), axis=1))
    owned_length = lax.optimization_barrier(jnp.sum(jnp.where(branch_ids[None, :] == owned[:, None], branch_len[None, :], 0), axis=1))
    slot_ids = jnp.arange(slot_count, dtype=jnp.int32)
    branch_tags = jnp.where(slot_ids[None, :] < owned_length[:, None], root_count + owned[:, None], -1)
    return jnp.concatenate([pool_root, branch_tags.astype(jnp.int32)], axis=1).reshape(-1)

def device_attention(index, fresh_queries, fresh_keys, fresh_values, cached_keys, cached_values, tags, token_request, request_branch, branch_root):
    query_groups = QUERY_HEADS // KEY_VALUE_HEADS
    begin_index = index * TOKENS_PER_SEQ
    query_rows = lax.dynamic_slice_in_dim(fresh_queries, begin_index, TOKENS_PER_SEQ, 0).astype(jnp.float32).reshape(TOKENS_PER_SEQ, KEY_VALUE_HEADS, query_groups, HEAD_SIZE)
    incoming_keys = lax.dynamic_slice_in_dim(fresh_keys, begin_index, TOKENS_PER_SEQ, 0).astype(jnp.float32).reshape(TOKENS_PER_SEQ, KEY_VALUE_HEADS, HEAD_SIZE)
    incoming_values = lax.dynamic_slice_in_dim(fresh_values, begin_index, TOKENS_PER_SEQ, 0).astype(jnp.float32).reshape(TOKENS_PER_SEQ, KEY_VALUE_HEADS, HEAD_SIZE)
    requests = lax.dynamic_index_in_dim(token_request, index, 0, keepdims=False)
    branches_here = lax.dynamic_index_in_dim(request_branch, index, 0, keepdims=False)
    token_branch = jnp.take(branches_here, requests)
    token_root = jnp.take(branch_root, token_branch)
    all_keys = jnp.concatenate([cached_keys, incoming_keys], axis=0)
    all_values = jnp.concatenate([cached_values, incoming_values], axis=0)
    scores = jnp.einsum('tkgd,rkd->tkgr', query_rows, all_keys) * HEAD_SIZE ** (-0.5)
    pool_seen = (tags[None, :] == token_root[:, None]) | (tags[None, :] == ROOTS + token_branch[:, None])
    positions = jnp.arange(TOKENS_PER_SEQ, dtype=jnp.int32)
    own_seen = (requests[None, :] == requests[:, None]) & (positions[None, :] <= positions[:, None])
    seen = jnp.concatenate([pool_seen, own_seen], axis=1)[:, None, None, :]
    peak = lax.optimization_barrier(jnp.max(jnp.where(seen, scores, -jnp.inf), axis=-1, keepdims=True))
    prob = jnp.where(seen, jnp.exp(scores - peak), 0.0)
    total = lax.optimization_barrier(jnp.sum(prob, axis=-1))
    weight = prob.astype(jnp.bfloat16).astype(jnp.float32)
    mixed = jnp.einsum('tkgr,rkd->tkgd', weight, all_values) / total[..., None]
    return mixed.reshape(TOKENS_PER_SEQ, QUERY_HEADS * HEAD_SIZE).astype(jnp.bfloat16)

def reference(fresh_queries, fresh_keys, fresh_values, cache, pool_root, branch_owner, branch_len, branch_root, request_branch, token_request, residual, wo_t, norm_gain, w_qkv):
    tags = cache_tags(pool_root, branch_owner, branch_len, ROOTS, BRANCH_CAP)
    cached_keys = cache[0].astype(jnp.float32).reshape(CACHED_ROWS, KEY_VALUE_HEADS, HEAD_SIZE)
    cached_values = cache[1].astype(jnp.float32).reshape(CACHED_ROWS, KEY_VALUE_HEADS, HEAD_SIZE)

    def one_device(index):
        return device_attention(index, fresh_queries, fresh_keys, fresh_values, cached_keys, cached_values, tags, token_request, request_branch, branch_root)
    blocks = lax.map(one_device, jnp.arange(N_SEQ, dtype=jnp.int32))
    attn = blocks.reshape(NEW_TOKENS, QUERY_HEADS * HEAD_SIZE)
    projected = lax.dot_general(attn, wo_t, (((1,), (1,)), ((), ())), preferred_element_type=jnp.float32)
    stream = (residual.astype(jnp.float32) + projected).astype(jnp.bfloat16)
    widened = stream.astype(jnp.float32)
    mean_square = lax.optimization_barrier(jnp.mean(widened * widened, axis=-1, keepdims=True))
    normed = (widened * lax.rsqrt(mean_square + 1e-06) * norm_gain[None, :]).astype(jnp.bfloat16)
    qkv_next = jnp.dot(normed, w_qkv, preferred_element_type=jnp.float32).astype(jnp.bfloat16)
    return (attn, stream, qkv_next)
```

```python
import math

import jax
import jax.numpy as jnp
from jax import lax
from jax.experimental import pallas as pl
from jax.experimental.pallas import tpu as pltpu
from jax.sharding import PartitionSpec as P

HEAD = 128
RING = 8
HALFRING = RING // 2
ROOTS = 32
ROWS = 160
NEG = -1e30
MESH = pl.DeviceIdType.MESH
F32 = jnp.float32
BF16 = jnp.bfloat16


def kernel(
    q_ref, fk_ref, fv_ref, cache_ref, pool_ref, owner_ref, len_ref, broot_ref, rb_ref, tr_ref,
    res_ref, wo_ref, gain_ref, wq_ref,
    attn_ref, stream_ref, qkv_ref,
    kvg, wqg, qb, s3, mx, mrun, acc, tags, tagc, rootb, brb, part, rsb, normed, qacc,
    send1, send2, recv1, recv2, part1, part2, xsend, xrecv,
):
    seq = lax.axis_index("seq")
    x = lax.axis_index("mp")
    y, z, c = seq // 16, (seq // 2) % RING, seq % 2
    scale2 = HEAD ** (-0.5) * math.log2(math.e)

    def dev(yy, zz, cc):
        return {"seq": (yy * RING + zz) * 2 + cc}

    def xdev(xx):
        return {"mp": xx}

    mate = dev(y, z, 1 - c)
    sec = (z, y)
    prim = (y, z)

    def place(h, ss, pp):
        return (pp, ss) if h == 0 else (ss, pp)

    def at(h, ss, pp):
        yy, zz = place(h, ss, pp)
        return dev(yy, zz, c)

    barrier = pltpu.get_barrier_semaphore()

    def greet(d, carry):
        pl.semaphore_signal(barrier, inc=1, device_id=dev((y + d) % RING, z, c), device_id_type=MESH)
        pl.semaphore_signal(barrier, inc=1, device_id=dev(y, (z + d) % RING, c), device_id_type=MESH)
        return carry

    lax.fori_loop(1, RING, greet, 0)
    pl.semaphore_signal(barrier, inc=1, device_id=mate, device_id_type=MESH)
    for d in range(1, 4):
        pl.semaphore_signal(barrier, inc=1, device_id=xdev((x + d) % 4), device_id_type=MESH)

    for h in range(2):
        kvg[h, seq, 0:64, :] = cache_ref[0, :, h * HEAD:(h + 1) * HEAD]
        kvg[h, seq, 64:128, :] = cache_ref[1, :, h * HEAD:(h + 1) * HEAD]
        for g in range(2):
            j = 2 * h + g
            kvg[h, seq, 128 + 16 * g:144 + 16 * g, :] = wo_ref[:, j * HEAD:(j + 1) * HEAD]
            qb[h, g * 64:(g + 1) * 64, :] = q_ref[:, j * HEAD:(j + 1) * HEAD]
        wqg[h, seq] = wq_ref[:, h * 512:(h + 1) * 512]

    e_id = lax.broadcasted_iota(jnp.int32, (128, 128), 0)
    b_id = lax.broadcasted_iota(jnp.int32, (128, 128), 1)
    owns = owner_ref[...] == e_id
    owned = jnp.sum(jnp.where(owns, b_id.astype(F32), 0.0), axis=1, keepdims=True)
    olen = jnp.sum(jnp.where(owns, len_ref[...].astype(F32), 0.0), axis=1, keepdims=True)
    slot = lax.broadcasted_iota(jnp.int32, (128, 32), 1).astype(F32)
    btag = jnp.where(slot < olen, ROOTS + owned, -1.0)
    pool = pool_ref[...].astype(F32)
    tags[...] = jnp.concatenate([pool, btag, pool, btag], axis=1)
    even = tags[pl.ds(0, 64, stride=2), :]
    odd = tags[pl.ds(1, 64, stride=2), :]
    lane = lax.broadcasted_iota(jnp.int32, (64, 128), 1)
    tagc[...] = jnp.where(lane < 64, even, odd)

    pl.semaphore_wait(barrier, 2 * (RING - 1) + 1 + 3)

    def copy1(h, yy, zz, cc, sem, to):
        ref = kvg.at[h, (yy * RING + zz) * 2 + cc]
        return pltpu.make_async_remote_copy(
            src_ref=ref, dst_ref=ref, send_sem=send1.at[h], recv_sem=sem.at[h, yy, zz],
            device_id=to, device_id_type=MESH)

    def copy2(h, yy, zz, cc, sem, to):
        ref = wqg.at[h, (yy * RING + zz) * 2 + cc]
        return pltpu.make_async_remote_copy(
            src_ref=ref, dst_ref=ref, send_sem=send2.at[h], recv_sem=sem.at[h, yy, zz],
            device_id=to, device_id_type=MESH)

    def inject(copy, rsem, psem, h, pp):
        yy, zz = place(h, sec[h], pp)
        copy(h, yy, zz, c, rsem, at(h, (sec[h] + 1) % RING, prim[h])).start()
        copy(h, yy, zz, c, rsem, at(h, (sec[h] + RING - 1) % RING, prim[h])).start()
        copy(h, yy, zz, c, psem, mate).start()

    def first(copy, rsem):
        def body(d, carry):
            for h in range(2):
                copy(h, y, z, c, rsem, at(h, sec[h], (prim[h] + d) % RING)).start()
            return carry
        return body

    lax.fori_loop(1, RING, first(copy1, recv1), 0)
    for h in range(2):
        inject(copy1, recv1, part1, h, prim[h])
    lax.fori_loop(1, RING, first(copy2, recv2), 0)

    tr = tr_ref[...].astype(F32)
    t_id = lax.broadcasted_iota(jnp.int32, (64, 64), 0)
    u_id = lax.broadcasted_iota(jnp.int32, (64, 64), 1)
    trc = jnp.sum(jnp.where(t_id == u_id, tr, 0.0), axis=1, keepdims=True)
    rb = rb_ref[...].astype(F32)
    tb = jnp.zeros((64, 1), F32)
    for r in range(4):
        tb = jnp.where(trc == float(r), rb[:, r:r + 1], tb)
    troot = jnp.sum(
        jnp.where(tb == lane.astype(F32), broot_ref[...].astype(F32), 0.0), axis=1, keepdims=True)
    rootb[...] = jnp.broadcast_to(troot, (64, 128))
    brb[...] = jnp.broadcast_to(tb + ROOTS, (64, 128))
    own_seen = (tr == trc) & (u_id <= t_id)
    own_seen2 = jnp.concatenate([own_seen.astype(F32), own_seen.astype(F32)], axis=0) > 0.5
    ones64 = jnp.ones((64, HEAD), BF16)
    for h in range(2):
        s = lax.dot_general(
            qb[h], fk_ref[:, h * HEAD:(h + 1) * HEAD], (((1,), (1,)), ((), ())),
            preferred_element_type=F32)
        s = jnp.where(own_seen2, s, NEG)
        m = jnp.max(s, axis=1, keepdims=True)
        p = jnp.exp2((s - m) * scale2).astype(BF16)
        v = jnp.concatenate([fv_ref[:, h * HEAD:(h + 1) * HEAD], ones64], axis=1)
        acc[h] = jnp.dot(p, v, preferred_element_type=F32)
        mrun[h] = jnp.broadcast_to(m, (128, 128))
        mx[h] = jnp.full((128, 128), NEG, F32)

    def wait_same(copy, rsem, h, yy, zz):
        copy(h, yy, zz, c, rsem, mate).wait_recv()

    def wait_mate(copy, psem, h, yy, zz):
        copy(h, yy, zz, 1 - c, psem, mate).wait_recv()

    def inject_rest(copy, rsem, psem):
        def body(i, carry):
            d = jnp.where(i % 2 == 1, (i + 1) // 2, RING - i // 2)
            for h in range(2):
                pp = (prim[h] + d) % RING
                yy, zz = place(h, sec[h], pp)
                wait_same(copy, rsem, h, yy, zz)
                inject(copy, rsem, psem, h, pp)
            return carry
        return body

    lax.fori_loop(1, RING, inject_rest(copy1, recv1, part1), 0)

    def relay(copy, rsem, psem, step, b):
        for h in range(2):
            if step == HALFRING:
                yy, zz = place(h, (sec[h] + HALFRING) % RING, b)
                wait_same(copy, rsem, h, yy, zz)
                copy(h, yy, zz, c, psem, mate).start()
                continue
            for way in (1, -1):
                yy, zz = place(h, (sec[h] - way * step + RING) % RING, b)
                wait_same(copy, rsem, h, yy, zz)
                onward = at(h, (sec[h] + way + RING) % RING, prim[h])
                if step < HALFRING - 1:
                    copy(h, yy, zz, c, rsem, onward).start()
                else:
                    @pl.when(b % 2 == (0 if way == 1 else 1))
                    def _():
                        copy(h, yy, zz, c, rsem, onward).start()
                copy(h, yy, zz, c, psem, mate).start()

    def bundle(h, step, b):
        if step == 0:
            return [place(h, sec[h], b)]
        if step == HALFRING:
            return [place(h, (sec[h] + HALFRING) % RING, b)]
        return [place(h, (sec[h] - step + RING) % RING, b), place(h, (sec[h] + step) % RING, b)]

    def qk(step, b):
        for h in range(2):
            slots = bundle(h, step, b)
            keys = []
            for yy, zz in slots:
                wait_mate(copy1, part1, h, yy, zz)
            for yy, zz in slots:
                keys.append(kvg[h, pl.ds((yy * RING + zz) * 2, 2), 0:64, :].reshape(128, HEAD))
            k = jnp.concatenate(keys, axis=0) if len(keys) > 1 else keys[0]
            s = lax.dot_general(qb[h], k, (((1,), (1,)), ((), ())), preferred_element_type=F32)
            top = mx[h]
            for i, (yy, zz) in enumerate(slots):
                tag = tagc[pl.ds(yy * RING + zz, 1), :]
                seen = (tag == rootb[...]) | (tag == brb[...])
                si = s[:, i * 128:(i + 1) * 128]
                lo = jnp.where(seen, si[0:64], NEG)
                hi = jnp.where(seen, si[64:128], NEG)
                si = jnp.concatenate([lo, hi], axis=0)
                s3[h, yy, zz] = si
                top = jnp.maximum(top, si)
            mx[h] = top

    def settle():
        for h in range(2):
            old = mrun[h]
            new = jnp.maximum(old, jnp.max(mx[h], axis=1, keepdims=True))
            factor = jnp.exp2((old - new) * scale2)
            mrun[h] = new
            acc[h] = acc[h] * jnp.concatenate([factor, factor], axis=1)

    def pv(step, b):
        for h in range(2):
            slots = bundle(h, step, b)
            m = mrun[h]
            ps, vs = [], []
            for yy, zz in slots:
                ps.append(jnp.exp2((s3[h, yy, zz] - m) * scale2).astype(BF16))
                vs.append(kvg[h, pl.ds((yy * RING + zz) * 2, 2), 64:128, :].reshape(128, HEAD))
            p = jnp.concatenate(ps, axis=1) if len(ps) > 1 else ps[0]
            v = jnp.concatenate(vs, axis=0) if len(vs) > 1 else vs[0]
            v = jnp.concatenate([v, jnp.ones(v.shape, BF16)], axis=1)
            acc[h] += jnp.dot(p, v, preferred_element_type=F32)

    def stage(relays, qk_step, pv_step):
        def body(b, carry):
            if relays is not None:
                relay(*relays, b)
            if qk_step is not None:
                qk(qk_step, b)
            if pv_step is not None:
                pv(pv_step, b)
            return carry
        lax.fori_loop(0, RING, body, 0)

    one = (copy1, recv1, part1)
    two = (copy2, recv2, part2)
    stage((*one, 1), 0, None)
    settle()
    stage((*one, 2), 1, 0)
    settle()
    stage((*one, 3), 2, 1)
    settle()
    for h in range(2):
        inject(*two, h, prim[h])
    lax.fori_loop(1, RING, inject_rest(*two), 0)
    stage((*one, 4), 3, 2)
    settle()
    stage((*two, 1), 4, 3)
    settle()
    stage((*two, 2), None, 4)

    for h in range(2):
        a = (acc[h, :, 0:HEAD] / acc[h, :, HEAD:2 * HEAD]).astype(BF16)
        for g in range(2):
            j = 2 * h + g
            attn_ref[:, j * HEAD:(j + 1) * HEAD] = a[g * 64:(g + 1) * 64]

    def project(yy, carry):
        w = [kvg[h, pl.ds(yy * 16, 16), 128 + 16 * g:144 + 16 * g, :].reshape(256, HEAD)
             for h in range(2) for g in range(2)]
        t = lax.dot_general(
            attn_ref[...], jnp.concatenate(w, axis=1), (((1,), (1,)), ((), ())),
            preferred_element_type=F32)
        part[:, pl.ds(pl.multiple_of(yy * 256, 256), 256)] = t.astype(BF16)
        return carry

    lax.fori_loop(0, RING, project, 0)

    def rows(xx):
        return pl.ds(pl.multiple_of(xx * 16, 16), 16)

    def scatter(d):
        xx = (x + d) % 4
        return pltpu.make_async_remote_copy(
            src_ref=part.at[rows(xx)], dst_ref=rsb.at[4 - d - 1], send_sem=xsend.at[0, d - 1],
            recv_sem=xrecv.at[0, 4 - d - 1], device_id=xdev(xx), device_id_type=MESH)

    for d in (2, 1, 3):
        scatter(d).start()
    stage((*two, 3), None, None)
    total = part[rows(x), :].astype(F32)
    for d in range(1, 4):
        scatter(4 - d).wait_recv()
        total = total + rsb[d - 1].astype(F32)
    stream_ref[rows(x), :] = (res_ref[rows(x), :].astype(F32) + total).astype(BF16)

    def spread(d, xx):
        return pltpu.make_async_remote_copy(
            src_ref=stream_ref.at[rows(xx)], dst_ref=stream_ref.at[rows(xx)],
            send_sem=xsend.at[1, d - 1], recv_sem=xrecv.at[1, 4 - d - 1],
            device_id=xdev((x + d) % 4), device_id_type=MESH)

    for d in (2, 1, 3):
        spread(d, x).start()
    stage((*two, 4), None, None)
    for d in range(1, 4):
        spread(4 - d, (x + d) % 4).wait_recv()

    wide = stream_ref[...].astype(F32)
    mean = jnp.mean(wide * wide, axis=1, keepdims=True)
    normed[...] = (wide * lax.rsqrt(mean + 1e-06) * gain_ref[...]).astype(BF16)
    qacc[...] = jnp.zeros_like(qacc)

    def qkv(yy, carry):
        n = normed[:, pl.ds(pl.multiple_of(yy * 256, 256), 256)]
        for h in range(2):
            for zz in range(RING):
                wait_mate(copy2, part2, h, yy, zz)
            qacc[:, h * 512:(h + 1) * 512] += jnp.dot(
                n, wqg[h, pl.ds(yy * 16, 16)].reshape(256, 512), preferred_element_type=F32)
        return carry

    lax.fori_loop(0, RING, qkv, 0)
    qkv_ref[...] = qacc[...].astype(BF16)

    for d in range(1, 4):
        scatter(d).wait_send()
        spread(d, x).wait_send()
    for h in range(2):
        for buf, sem in ((kvg, send1), (wqg, send2)):
            sent = buf.at[h, 0:127]
            pltpu.make_async_remote_copy(
                src_ref=sent, dst_ref=sent, send_sem=sem.at[h], recv_sem=recv1.at[h, 0, 0],
                device_id=mate, device_id_type=MESH).wait_send()


def on_device(
    fresh_queries, fresh_keys, fresh_values, cache, pool_root, branch_owner, branch_len,
    branch_root, request_branch, token_request, residual, wo_t, norm_gain, w_qkv,
):
    vmem = pl.BlockSpec(memory_space=pltpu.VMEM)
    args = (
        fresh_queries, fresh_keys, fresh_values, cache, pool_root, branch_owner.reshape(1, -1),
        branch_len.reshape(1, -1), branch_root.reshape(1, -1), request_branch, token_request,
        residual, wo_t, norm_gain.reshape(1, -1), w_qkv,
    )
    dma = pltpu.SemaphoreType.DMA
    return pl.pallas_call(
        kernel,
        out_shape=(
            jax.ShapeDtypeStruct((64, 512), BF16),
            jax.ShapeDtypeStruct((64, 2048), BF16),
            jax.ShapeDtypeStruct((64, 1024), BF16),
        ),
        in_specs=[vmem] * len(args),
        out_specs=(vmem, vmem, vmem),
        scratch_shapes=[
            pltpu.VMEM((2, 2 * RING * RING, ROWS, HEAD), BF16),
            pltpu.VMEM((2, 2 * RING * RING, 16, 512), BF16),
            pltpu.VMEM((2, 128, HEAD), BF16),
            pltpu.VMEM((2, RING, RING, 128, 128), F32),
            pltpu.VMEM((2, 128, 128), F32),
            pltpu.VMEM((2, 128, 128), F32),
            pltpu.VMEM((2, 128, 256), F32),
            pltpu.VMEM((128, 128), F32),
            pltpu.VMEM((64, 128), F32),
            pltpu.VMEM((64, 128), F32),
            pltpu.VMEM((64, 128), F32),
            pltpu.VMEM((64, 2048), BF16),
            pltpu.VMEM((3, 16, 2048), BF16),
            pltpu.VMEM((64, 2048), BF16),
            pltpu.VMEM((64, 1024), F32),
            dma((2,)),
            dma((2,)),
            dma((2, RING, RING)),
            dma((2, RING, RING)),
            dma((2, RING, RING)),
            dma((2, RING, RING)),
            dma((2, 3)),
            dma((2, 3)),
        ],
        compiler_params=pltpu.CompilerParams(
            collective_id=0, has_side_effects=True, vmem_limit_bytes=60 * 1024 * 1024),
    )(*args)


def solution(mesh):
    return jax.shard_map(
        on_device,
        mesh=mesh,
        in_specs=(
            P("seq", "mp"),
            P("seq", "mp"),
            P("seq", "mp"),
            P(None, "seq", "mp"),
            P(),
            P(),
            P(),
            P(),
            P("seq", None),
            P("seq", None),
            P("seq", None),
            P("seq", "mp"),
            P(),
            P("seq", "mp"),
        ),
        out_specs=(P("seq", "mp"), P("seq", None), P("seq", "mp")),
        check_vma=False,
    )
```

```python
import math

import jax
import jax.numpy as jnp
from jax import lax
from jax.experimental import pallas as pl
from jax.experimental.pallas import tpu as pltpu
from jax.sharding import PartitionSpec as P

HEAD = 128
RING = 8
HALFRING = RING // 2
ROOTS = 32
ROWS = 160
NEG = -1e30
FLOOR = -1e9
MESH = pl.DeviceIdType.MESH
F32 = jnp.float32
BF16 = jnp.bfloat16


def kernel(
    q_ref, fk_ref, fv_ref, cache_ref, pool_ref, owner_ref, len_ref, broot_ref, rb_ref, tr_ref,
    res_ref, wo_ref, gain_ref, wq_ref,
    attn_ref, stream_ref, qkv_ref,
    kvg, wqg, qb, tok, s3, mx, mrun, acc, tags, box, part, rsb, normed, qacc,
    send1, send2, sendm, recv1, recv2, part1, part2, xsend, xrecv, swap,
):
    seq = lax.axis_index("seq")
    x = lax.axis_index("mp")
    y, z, c = seq // 16, (seq // 2) % RING, seq % 2
    scale2 = HEAD ** (-0.5) * math.log2(math.e)

    def dev(yy, zz, cc):
        return {"seq": (yy * RING + zz) * 2 + cc}

    def xdev(xx):
        return {"mp": xx}

    mate = dev(y, z, 1 - c)
    sec = (z, y)
    prim = (y, z)

    def place(h, ss, pp):
        return (pp, ss) if h == 0 else (ss, pp)

    def at(h, ss, pp):
        yy, zz = place(h, ss, pp)
        return dev(yy, zz, c)

    barrier = pltpu.get_barrier_semaphore()

    for d in (1, RING - 1):
        pl.semaphore_signal(barrier, inc=1, device_id=dev((y + d) % RING, z, c), device_id_type=MESH)
        pl.semaphore_signal(barrier, inc=1, device_id=dev(y, (z + d) % RING, c), device_id_type=MESH)
    pl.semaphore_signal(barrier, inc=1, device_id=mate, device_id_type=MESH)
    for d in range(1, 4):
        pl.semaphore_signal(barrier, inc=1, device_id=xdev((x + d) % 4), device_id_type=MESH)

    for h in range(2):
        kvg[h, seq, 0:64, :] = cache_ref[0, :, h * HEAD:(h + 1) * HEAD]
        kvg[h, seq, 64:128, :] = cache_ref[1, :, h * HEAD:(h + 1) * HEAD]
        for g in range(2):
            j = 2 * h + g
            kvg[h, seq, 128 + 16 * g:144 + 16 * g, :] = wo_ref[:, j * HEAD:(j + 1) * HEAD]
            qb[0, h, g * 64:(g + 1) * 64, :] = q_ref[:, j * HEAD:(j + 1) * HEAD]
        wqg[h, seq] = wq_ref[:, h * 512:(h + 1) * 512]

    e_id = lax.broadcasted_iota(jnp.int32, (128, 128), 0)
    b_id = lax.broadcasted_iota(jnp.int32, (128, 128), 1)
    owns = owner_ref[...] == e_id
    owned = jnp.sum(jnp.where(owns, b_id.astype(F32), 0.0), axis=1, keepdims=True)
    olen = jnp.sum(jnp.where(owns, len_ref[...].astype(F32), 0.0), axis=1, keepdims=True)
    slot = lax.broadcasted_iota(jnp.int32, (128, 32), 1).astype(F32)
    btag = jnp.where(slot < olen, ROOTS + owned, -1.0)
    pool = pool_ref[...].astype(F32).T
    tags[...] = jnp.concatenate([pool, btag, pool, btag], axis=1)
    lane = lax.broadcasted_iota(jnp.int32, (64, 128), 1)

    tr = tr_ref[...].astype(F32)
    t_id = lax.broadcasted_iota(jnp.int32, (64, 64), 0)
    u_id = lax.broadcasted_iota(jnp.int32, (64, 64), 1)
    trc = jnp.sum(jnp.where(t_id == u_id, tr, 0.0), axis=1, keepdims=True)
    rb = rb_ref[...].astype(F32)
    tb = jnp.zeros((64, 1), F32)
    for r in range(4):
        tb = jnp.where(trc == float(r), rb[:, r:r + 1], tb)
    troot = jnp.sum(
        jnp.where(tb == lane.astype(F32), broot_ref[...].astype(F32), 0.0), axis=1, keepdims=True)
    tok[0, 0] = jnp.broadcast_to(troot, (64, 128))
    tok[0, 1] = jnp.broadcast_to(tb + ROOTS, (64, 128))
    pl.semaphore_wait(barrier, 4 + 1 + 3)

    def copy1(h, yy, zz, cc, sem, to):
        ref = kvg.at[h, (yy * RING + zz) * 2 + cc]
        return pltpu.make_async_remote_copy(
            src_ref=ref, dst_ref=ref, send_sem=send1.at[h], recv_sem=sem.at[h, yy, zz],
            device_id=to, device_id_type=MESH)

    def copy2(h, yy, zz, cc, sem, to):
        ref = wqg.at[h, (yy * RING + zz) * 2 + cc]
        return pltpu.make_async_remote_copy(
            src_ref=ref, dst_ref=ref, send_sem=send2.at[h], recv_sem=sem.at[h, yy, zz],
            device_id=to, device_id_type=MESH)

    def share1(h, yy, zz, cc):
        ref = kvg.at[h, (yy * RING + zz) * 2 + cc, 128:ROWS]
        return pltpu.make_async_remote_copy(
            src_ref=ref, dst_ref=ref, send_sem=sendm.at[h], recv_sem=part1.at[h, yy, zz],
            device_id=mate, device_id_type=MESH)

    def share2(h, yy, zz, cc):
        return copy2(h, yy, zz, cc, part2, mate)

    def trade(i, mine, theirs):
        return pltpu.make_async_remote_copy(
            src_ref=mine, dst_ref=theirs, send_sem=swap.at[0, i], recv_sem=swap.at[1, i],
            device_id=mate, device_id_type=MESH)

    trades = [trade(0, qb.at[0], qb.at[1]), trade(1, tok.at[0], tok.at[1]), trade(2, box.at[0], box.at[1])]

    def inject(copy, rsem, share, h, pp):
        yy, zz = place(h, sec[h], pp)
        copy(h, yy, zz, c, rsem, at(h, (sec[h] + 1) % RING, prim[h])).start()
        copy(h, yy, zz, c, rsem, at(h, (sec[h] + RING - 1) % RING, prim[h])).start()
        share(h, yy, zz, c).start()

    def start_ring(copy, rsem):
        for h in range(2):
            for way in (1, RING - 1):
                copy(h, y, z, c, rsem, at(h, sec[h], (prim[h] + way) % RING)).start()

    start_ring(copy1, recv1)
    for h in range(2):
        inject(copy1, recv1, share1, h, prim[h])
    trades[0].start()
    trades[1].start()

    own_seen = (tr == trc) & (u_id <= t_id)
    own_seen2 = jnp.concatenate([own_seen.astype(F32), own_seen.astype(F32)], axis=0) > 0.5
    ones64 = jnp.ones((64, HEAD), BF16)
    for h in range(2):
        s = lax.dot_general(
            qb[0, h], fk_ref[:, h * HEAD:(h + 1) * HEAD], (((1,), (1,)), ((), ())),
            preferred_element_type=F32)
        s = jnp.where(own_seen2, s, NEG)
        m = jnp.max(s, axis=1, keepdims=True)
        p = jnp.exp2((s - m) * scale2).astype(BF16)
        v = jnp.concatenate([fv_ref[:, h * HEAD:(h + 1) * HEAD], ones64], axis=1)
        acc[h, 0:128] = jnp.dot(p, v, preferred_element_type=F32)
        acc[h, 128:256] = jnp.zeros((128, 256), F32)
        mrun[h, 0:128] = jnp.broadcast_to(m, (128, 128))
        mrun[h, 128:256] = jnp.full((128, 128), FLOOR, F32)
        mx[h] = jnp.full((256, 128), NEG, F32)

    def wait_same(copy, rsem, h, yy, zz):
        copy(h, yy, zz, c, rsem, mate).wait_recv()

    def ring(copy, rsem, step, after):
        for h in range(2):
            ways = (1, -1) if step < HALFRING else (1,)
            for way in ways:
                pp = (prim[h] - way * step + RING) % RING
                yy, zz = place(h, sec[h], pp)
                wait_same(copy, rsem, h, yy, zz)
                last = step == HALFRING - 1
                if step < HALFRING - 1 or (last and way == (1 if h == 0 else -1)):
                    copy(h, yy, zz, c, rsem, at(h, sec[h], (prim[h] + way + RING) % RING)).start()
                if after is not None:
                    after(h, pp)

    for step in range(1, HALFRING + 1):
        ring(copy1, recv1, step, lambda h, pp: inject(copy1, recv1, share1, h, pp))

    def near(h, i):
        d = jnp.where(i % 2 == 1, (i + 1) // 2, RING - i // 2)
        return (prim[h] + d) % RING

    def relay(copy, rsem, share, step, i):
        for h in range(2):
            b = near(h, i)
            if step == HALFRING:
                yy, zz = place(h, (sec[h] + HALFRING) % RING, b)
                wait_same(copy, rsem, h, yy, zz)
                share(h, yy, zz, c).start()
                continue
            for way in (1, -1):
                yy, zz = place(h, (sec[h] - way * step + RING) % RING, b)
                wait_same(copy, rsem, h, yy, zz)
                onward = at(h, (sec[h] + way + RING) % RING, prim[h])
                if step < HALFRING - 1:
                    copy(h, yy, zz, c, rsem, onward).start()
                else:
                    @pl.when(i % 2 == (0 if way == 1 else 1))
                    def _():
                        copy(h, yy, zz, c, rsem, onward).start()
                share(h, yy, zz, c).start()

    def bundle(h, step, i):
        if step in (0, HALFRING):
            ss = (sec[h] + step) % RING
            return [place(h, ss, near(h, 2 * i)), place(h, ss, near(h, 2 * i + 1))]
        b = near(h, i)
        return [place(h, (sec[h] - step + RING) % RING, b), place(h, (sec[h] + step) % RING, b)]

    def held(h, slots, begin):
        return jnp.concatenate(
            [kvg[h, (yy * RING + zz) * 2 + c, begin:begin + 64, :] for yy, zz in slots], axis=0)

    half_lane = lax.broadcasted_iota(jnp.int32, (1, 128), 1) < 64

    def qk(step, i):
        for h in range(2):
            slots = bundle(h, step, i)
            q = jnp.concatenate([qb[0, h], qb[1, h]], axis=0)
            s = lax.dot_general(
                q, held(h, slots, 0), (((1,), (1,)), ((), ())), preferred_element_type=F32)
            a, b = [tags[pl.ds((yy * RING + zz) * 2 + c, 1), :] for yy, zz in slots]
            tag = jnp.where(half_lane, a, b)
            parts = []
            for k in range(2):
                seen = (tag == tok[k, 0]) | (tag == tok[k, 1])
                for g in range(2):
                    r = 128 * k + 64 * g
                    parts.append(jnp.where(seen, s[r:r + 64], NEG))
            s = jnp.concatenate(parts, axis=0)
            s3[h, step * RING + i] = s
            mx[h] = jnp.maximum(mx[h], s)

    def settle():
        for h in range(2):
            old = mrun[h]
            new = jnp.maximum(old, jnp.max(mx[h], axis=1, keepdims=True))
            factor = jnp.exp2((old - new) * scale2)
            mrun[h] = new
            acc[h] = acc[h] * jnp.concatenate([factor, factor], axis=1)

    ones128 = jnp.ones((128, HEAD), BF16)

    def pv(step, i):
        for h in range(2):
            p = jnp.exp2((s3[h, step * RING + i] - mrun[h]) * scale2).astype(BF16)
            v = jnp.concatenate([held(h, bundle(h, step, i), 64), ones128], axis=1)
            acc[h] += jnp.dot(p, v, preferred_element_type=F32)

    def stage(relays, qk_step, pv_step, begin=0, end=RING):
        def body(b, carry):
            if relays is not None:
                relay(*relays, b)
            if qk_step is not None:
                qk(qk_step, b)
            if pv_step is not None:
                pv(pv_step, b)
            return carry
        lax.fori_loop(begin, end, body, 0)

    one = (copy1, recv1, share1)
    two = (copy2, recv2, share2)
    start_ring(copy2, recv2)
    trades[0].wait_recv()
    trades[1].wait_recv()
    stage((*one, 1), 0, None, 0, 4)
    stage((*one, 1), None, None, 4, RING)
    settle()
    ring(copy2, recv2, 1, None)
    stage((*one, 2), 1, 0, 0, 4)
    stage((*one, 2), 1, None, 4, RING)
    settle()
    ring(copy2, recv2, 2, None)
    stage((*one, 3), 2, 1, 0, 4)
    ring(copy2, recv2, 3, None)
    stage((*one, 3), 2, 1, 4, RING)
    settle()
    ring(copy2, recv2, 4, None)

    def inject_all(i, carry):
        for h in range(2):
            inject(*two, h, near(h, i))
        return carry

    lax.fori_loop(0, RING, inject_all, 0)
    stage((*one, 4), 3, 2)
    settle()
    stage((*two, 1), 4, 3, 0, 4)
    stage((*two, 1), None, 3, 4, RING)
    settle()
    stage(None, None, 4, 0, 4)

    lane2 = lax.broadcasted_iota(jnp.int32, (128, 128), 1) < 64
    for h in range(2):
        box[0, h, :, 0:HEAD] = acc[h, 128:256, 0:HEAD]
        box[0, h, :, HEAD:] = jnp.where(lane2, mrun[h, 128:256], acc[h, 128:256, HEAD:])
    trades[2].start()
    stage((*two, 2), None, None)
    trades[2].wait_recv()
    for h in range(2):
        m_here = mrun[h, 0:128]
        m_there = box[1, h, :, HEAD:HEAD + 1]
        top = jnp.maximum(m_here, m_there)
        w_here = jnp.exp2((m_here - top) * scale2)
        w_there = jnp.exp2((m_there - top) * scale2)
        mixed = acc[h, 0:128, 0:HEAD] * w_here + box[1, h, :, 0:HEAD] * w_there
        total = acc[h, 0:128, HEAD:] * w_here + box[1, h, :, 2 * HEAD - 1:2 * HEAD] * w_there
        a = (mixed / total).astype(BF16)
        for g in range(2):
            j = 2 * h + g
            attn_ref[:, j * HEAD:(j + 1) * HEAD] = a[g * 64:(g + 1) * 64]

    def project(yy, carry):
        for h in range(2):
            for zz in range(RING):
                share1(h, yy, zz, 1 - c).wait_recv()
        w = [kvg[h, pl.ds(yy * 16, 16), 128 + 16 * g:144 + 16 * g, :].reshape(256, HEAD)
             for h in range(2) for g in range(2)]
        t = lax.dot_general(
            attn_ref[...], jnp.concatenate(w, axis=1), (((1,), (1,)), ((), ())),
            preferred_element_type=F32)
        part[:, pl.ds(pl.multiple_of(yy * 256, 256), 256)] = t.astype(BF16)
        return carry

    lax.fori_loop(0, RING, project, 0)

    def rows(xx):
        return pl.ds(pl.multiple_of(xx * 16, 16), 16)

    def scatter(d):
        xx = (x + d) % 4
        return pltpu.make_async_remote_copy(
            src_ref=part.at[rows(xx)], dst_ref=rsb.at[4 - d - 1], send_sem=xsend.at[0, d - 1],
            recv_sem=xrecv.at[0, 4 - d - 1], device_id=xdev(xx), device_id_type=MESH)

    for d in (2, 1, 3):
        scatter(d).start()
    stage((*two, 3), None, None)
    total = part[rows(x), :].astype(F32)
    for d in range(1, 4):
        scatter(4 - d).wait_recv()
        total = total + rsb[d - 1].astype(F32)
    stream_ref[rows(x), :] = (res_ref[rows(x), :].astype(F32) + total).astype(BF16)

    def spread(d, xx):
        return pltpu.make_async_remote_copy(
            src_ref=stream_ref.at[rows(xx)], dst_ref=stream_ref.at[rows(xx)],
            send_sem=xsend.at[1, d - 1], recv_sem=xrecv.at[1, 4 - d - 1],
            device_id=xdev((x + d) % 4), device_id_type=MESH)

    for d in (2, 1, 3):
        spread(d, x).start()
    stage((*two, 4), None, None)
    for d in range(1, 4):
        spread(4 - d, (x + d) % 4).wait_recv()

    wide = stream_ref[...].astype(F32)
    mean = jnp.mean(wide * wide, axis=1, keepdims=True)
    normed[...] = (wide * lax.rsqrt(mean + 1e-06) * gain_ref[...]).astype(BF16)
    qacc[...] = jnp.zeros_like(qacc)

    def qkv(yy, carry):
        n = normed[:, pl.ds(pl.multiple_of(yy * 256, 256), 256)]
        for h in range(2):
            for zz in range(RING):
                share2(h, yy, zz, 1 - c).wait_recv()
            qacc[:, h * 512:(h + 1) * 512] += jnp.dot(
                n, wqg[h, pl.ds(yy * 16, 16)].reshape(256, 512), preferred_element_type=F32)
        return carry

    lax.fori_loop(0, RING, qkv, 0)
    qkv_ref[...] = qacc[...].astype(BF16)

    for d in range(1, 4):
        scatter(d).wait_send()
        spread(d, x).wait_send()
    for t in trades:
        t.wait_send()

    def drain(sent, sem):
        pltpu.make_async_remote_copy(
            src_ref=sent, dst_ref=sent, send_sem=sem, recv_sem=recv1.at[0, 0, 0],
            device_id=mate, device_id_type=MESH).wait_send()

    for h in range(2):
        drain(kvg.at[h, 0:63], send1.at[h])
        drain(kvg.at[h, 0:64, 128:ROWS], sendm.at[h])
        drain(wqg.at[h, 0:127], send2.at[h])


def hand_out(*refs):
    sources, results, held, sem = refs[0:3], refs[3:6], refs[6:9], refs[9]
    ins = [pltpu.make_async_copy(sources[i], held[i], sem.at[i]) for i in range(3)]
    outs = [pltpu.make_async_copy(held[i], results[i], sem.at[3 + i]) for i in range(3)]
    for copy in ins:
        copy.start()
    for i in range(3):
        ins[i].wait()
        outs[i].start()
    for copy in outs:
        copy.wait()


def on_device(
    fresh_queries, fresh_keys, fresh_values, cache, pool_root, branch_owner, branch_len,
    branch_root, request_branch, token_request, residual, wo_t, norm_gain, w_qkv,
):
    vmem = pl.BlockSpec(memory_space=pltpu.VMEM)
    args = (
        fresh_queries, fresh_keys, fresh_values, cache, pool_root.T, branch_owner.reshape(1, -1),
        branch_len.reshape(1, -1), branch_root.reshape(1, -1), request_branch, token_request,
        residual, wo_t, norm_gain.reshape(1, -1), w_qkv,
    )
    dma = pltpu.SemaphoreType.DMA
    shapes = tuple(jax.ShapeDtypeStruct((64, width), BF16) for width in (512, 2048, 1024))
    results = pl.pallas_call(
        kernel,
        out_shape=shapes,
        in_specs=[vmem] * len(args),
        out_specs=(vmem, vmem, vmem),
        scratch_shapes=[
            pltpu.VMEM((2, 2 * RING * RING, ROWS, HEAD), BF16),
            pltpu.VMEM((2, 2 * RING * RING, 16, 512), BF16),
            pltpu.VMEM((2, 2, 128, HEAD), BF16),
            pltpu.VMEM((2, 2, 64, 128), F32),
            pltpu.VMEM((2, 5 * RING, 256, 128), F32),
            pltpu.VMEM((2, 256, 128), F32),
            pltpu.VMEM((2, 256, 128), F32),
            pltpu.VMEM((2, 256, 256), F32),
            pltpu.VMEM((128, 128), F32),
            pltpu.VMEM((2, 2, 128, 256), F32),
            pltpu.VMEM((64, 2048), BF16),
            pltpu.VMEM((3, 16, 2048), BF16),
            pltpu.VMEM((64, 2048), BF16),
            pltpu.VMEM((64, 1024), F32),
            dma((2,)),
            dma((2,)),
            dma((2,)),
            dma((2, RING, RING)),
            dma((2, RING, RING)),
            dma((2, RING, RING)),
            dma((2, RING, RING)),
            dma((2, 3)),
            dma((2, 3)),
            dma((2, 3)),
        ],
        compiler_params=pltpu.CompilerParams(
            collective_id=0, has_side_effects=True, vmem_limit_bytes=60 * 1024 * 1024),
    )(*args)
    place = pl.BlockSpec(memory_space=pl.ANY)
    return pl.pallas_call(
        hand_out,
        out_shape=shapes,
        in_specs=[place] * 3,
        out_specs=(place,) * 3,
        scratch_shapes=[pltpu.VMEM(s.shape, BF16) for s in shapes] + [dma((6,))],
    )(*results)


def solution(mesh):
    return jax.shard_map(
        on_device,
        mesh=mesh,
        in_specs=(
            P("seq", "mp"),
            P("seq", "mp"),
            P("seq", "mp"),
            P(None, "seq", "mp"),
            P(),
            P(),
            P(),
            P(),
            P("seq", None),
            P("seq", None),
            P("seq", None),
            P("seq", "mp"),
            P(),
            P("seq", "mp"),
        ),
        out_specs=(P("seq", "mp"), P("seq", None), P("seq", "mp")),
        check_vma=False,
    )
```

```python
import math

import jax
import jax.numpy as jnp
from jax import lax
from jax.experimental import pallas as pl
from jax.experimental.pallas import tpu as pltpu
from jax.sharding import PartitionSpec as P

HEAD = 128
RING = 8
HALFRING = RING // 2
ROOTS = 32
ROWS = 160
NEG = -1e30
FLOOR = -1e9
MESH = pl.DeviceIdType.MESH
F32 = jnp.float32
BF16 = jnp.bfloat16


def kernel(
    q_ref, fk_ref, fv_ref, cache_ref, pool_ref, owner_ref, len_ref, broot_ref, rb_ref, tr_ref,
    res_ref, wo_ref, gain_ref, wq_ref,
    attn_ref, stream_ref, qkv_ref,
    kvg, wqg, qb, tok, s3, mx, mrun, acc, tags, box, part, rsb, normed, qacc,
    send1, send2, sendm, recv1, recv2, part1, part2, xsend, xrecv, swap,
):
    seq = lax.axis_index("seq")
    x = lax.axis_index("mp")
    y, z, c = seq // 16, (seq // 2) % RING, seq % 2
    scale2 = HEAD ** (-0.5) * math.log2(math.e)

    def dev(yy, zz, cc):
        return {"seq": (yy * RING + zz) * 2 + cc}

    def xdev(xx):
        return {"mp": xx}

    mate = dev(y, z, 1 - c)
    sec = (z, y)
    prim = (y, z)

    def place(h, ss, pp):
        return (pp, ss) if h == 0 else (ss, pp)

    def at(h, ss, pp):
        yy, zz = place(h, ss, pp)
        return dev(yy, zz, c)

    barrier = pltpu.get_barrier_semaphore()

    for d in (1, RING - 1):
        pl.semaphore_signal(barrier, inc=1, device_id=dev((y + d) % RING, z, c), device_id_type=MESH)
        pl.semaphore_signal(barrier, inc=1, device_id=dev(y, (z + d) % RING, c), device_id_type=MESH)
    pl.semaphore_signal(barrier, inc=1, device_id=mate, device_id_type=MESH)
    for d in range(1, 4):
        pl.semaphore_signal(barrier, inc=1, device_id=xdev((x + d) % 4), device_id_type=MESH)

    for h in range(2):
        kvg[h, seq, 0:64, :] = cache_ref[0, :, h * HEAD:(h + 1) * HEAD]
        kvg[h, seq, 64:128, :] = cache_ref[1, :, h * HEAD:(h + 1) * HEAD]
        for g in range(2):
            j = 2 * h + g
            kvg[h, seq, 128 + 16 * g:144 + 16 * g, :] = wo_ref[:, j * HEAD:(j + 1) * HEAD]

    pl.semaphore_wait(barrier, 4 + 1 + 3)

    def copy1(h, yy, zz, cc, sem, to):
        ref = kvg.at[h, (yy * RING + zz) * 2 + cc]
        return pltpu.make_async_remote_copy(
            src_ref=ref, dst_ref=ref, send_sem=send1.at[h], recv_sem=sem.at[h, yy, zz],
            device_id=to, device_id_type=MESH)

    def copy2(h, yy, zz, cc, sem, to):
        ref = wqg.at[h, (yy * RING + zz) * 2 + cc]
        return pltpu.make_async_remote_copy(
            src_ref=ref, dst_ref=ref, send_sem=send2.at[h], recv_sem=sem.at[h, yy, zz],
            device_id=to, device_id_type=MESH)

    def share1(h, yy, zz, cc):
        ref = kvg.at[h, (yy * RING + zz) * 2 + cc, 128:ROWS]
        return pltpu.make_async_remote_copy(
            src_ref=ref, dst_ref=ref, send_sem=sendm.at[h], recv_sem=part1.at[h],
            device_id=mate, device_id_type=MESH)

    def share2(h, yy, zz, cc):
        ref = wqg.at[h, (yy * RING + zz) * 2 + cc]
        return pltpu.make_async_remote_copy(
            src_ref=ref, dst_ref=ref, send_sem=sendm.at[2 + h], recv_sem=part2.at[h],
            device_id=mate, device_id_type=MESH)

    def trade(i, mine, theirs):
        return pltpu.make_async_remote_copy(
            src_ref=mine, dst_ref=theirs, send_sem=swap.at[0, i], recv_sem=swap.at[1, i],
            device_id=mate, device_id_type=MESH)

    trades = [trade(0, qb.at[0], qb.at[1]), trade(1, tok.at[0], tok.at[1]), trade(2, box.at[0, 0], box.at[1, 0]), trade(3, box.at[0, 1], box.at[1, 1])]

    def inject(copy, rsem, share, h, pp):
        yy, zz = place(h, sec[h], pp)
        copy(h, yy, zz, c, rsem, at(h, (sec[h] + 1) % RING, prim[h])).start()
        copy(h, yy, zz, c, rsem, at(h, (sec[h] + RING - 1) % RING, prim[h])).start()
        share(h, yy, zz, c).start()

    def start_ring(copy, rsem):
        for h in range(2):
            for way in (1, RING - 1):
                copy(h, y, z, c, rsem, at(h, sec[h], (prim[h] + way) % RING)).start()

    start_ring(copy1, recv1)
    for h in range(2):
        inject(copy1, recv1, share1, h, prim[h])

    for h in range(2):
        for g in range(2):
            j = 2 * h + g
            qb[0, h, g * 64:(g + 1) * 64, :] = q_ref[:, j * HEAD:(j + 1) * HEAD]
        wqg[h, seq] = wq_ref[:, h * 512:(h + 1) * 512]

    e_id = lax.broadcasted_iota(jnp.int32, (128, 128), 0)
    b_id = lax.broadcasted_iota(jnp.int32, (128, 128), 1)
    owns = owner_ref[...] == e_id
    owned = jnp.sum(jnp.where(owns, b_id.astype(F32), 0.0), axis=1, keepdims=True)
    olen = jnp.sum(jnp.where(owns, len_ref[...].astype(F32), 0.0), axis=1, keepdims=True)
    slot = lax.broadcasted_iota(jnp.int32, (128, 32), 1).astype(F32)
    btag = jnp.where(slot < olen, ROOTS + owned, -1.0)
    pool = pool_ref[...].astype(F32).T
    tags[...] = jnp.concatenate([pool, btag, pool, btag], axis=1)
    lane = lax.broadcasted_iota(jnp.int32, (64, 128), 1)

    tr = tr_ref[...].astype(F32)
    t_id = lax.broadcasted_iota(jnp.int32, (64, 64), 0)
    u_id = lax.broadcasted_iota(jnp.int32, (64, 64), 1)
    trc = jnp.sum(jnp.where(t_id == u_id, tr, 0.0), axis=1, keepdims=True)
    rb = rb_ref[...].astype(F32)
    tb = jnp.zeros((64, 1), F32)
    for r in range(4):
        tb = jnp.where(trc == float(r), rb[:, r:r + 1], tb)
    troot = jnp.sum(
        jnp.where(tb == lane.astype(F32), broot_ref[...].astype(F32), 0.0), axis=1, keepdims=True)
    tok[0, 0] = jnp.broadcast_to(troot, (64, 128))
    tok[0, 1] = jnp.broadcast_to(tb + ROOTS, (64, 128))
    trades[0].start()
    trades[1].start()


    own_seen = (tr == trc) & (u_id <= t_id)
    own_seen2 = jnp.concatenate([own_seen.astype(F32), own_seen.astype(F32)], axis=0) > 0.5
    ones64 = jnp.ones((64, HEAD), BF16)
    for h in range(2):
        s = lax.dot_general(
            qb[0, h], fk_ref[:, h * HEAD:(h + 1) * HEAD], (((1,), (1,)), ((), ())),
            preferred_element_type=F32)
        s = jnp.where(own_seen2, s, NEG)
        m = jnp.max(s, axis=1, keepdims=True)
        p = jnp.exp2((s - m) * scale2).astype(BF16)
        v = jnp.concatenate([fv_ref[:, h * HEAD:(h + 1) * HEAD], ones64], axis=1)
        acc[h, 0:128] = jnp.dot(p, v, preferred_element_type=F32)
        acc[h, 128:256] = jnp.zeros((128, 256), F32)
        mrun[h, 0:128] = jnp.broadcast_to(m, (128, 128))
        mrun[h, 128:256] = jnp.full((128, 128), FLOOR, F32)
        mx[h] = jnp.full((256, 128), NEG, F32)

    def wait_same(copy, rsem, h, yy, zz):
        copy(h, yy, zz, c, rsem, mate).wait_recv()

    def ring(copy, rsem, step, after):
        for h in range(2):
            ways = (1, -1) if step < HALFRING else (1,)
            for way in ways:
                pp = (prim[h] - way * step + RING) % RING
                yy, zz = place(h, sec[h], pp)
                wait_same(copy, rsem, h, yy, zz)
                last = step == HALFRING - 1
                if step < HALFRING - 1 or (last and way == (1 if h == 0 else -1)):
                    copy(h, yy, zz, c, rsem, at(h, sec[h], (prim[h] + way + RING) % RING)).start()
                if after is not None:
                    after(h, pp)

    def near(h, i):
        d = jnp.where(i % 2 == 1, (i + 1) // 2, RING - i // 2)
        return (prim[h] + d) % RING

    def relay(copy, rsem, share, step, i):
        for h in range(2):
            b = near(h, i)
            if step == HALFRING:
                yy, zz = place(h, (sec[h] + HALFRING) % RING, b)
                wait_same(copy, rsem, h, yy, zz)
                share(h, yy, zz, c).start()
                continue
            for way in (1, -1):
                yy, zz = place(h, (sec[h] - way * step + RING) % RING, b)
                wait_same(copy, rsem, h, yy, zz)
                onward = at(h, (sec[h] + way + RING) % RING, prim[h])
                if step < HALFRING - 1:
                    copy(h, yy, zz, c, rsem, onward).start()
                else:
                    @pl.when(i % 2 == (0 if way == 1 else 1))
                    def _():
                        copy(h, yy, zz, c, rsem, onward).start()
                share(h, yy, zz, c).start()

    one = (copy1, recv1, share1)
    two = (copy2, recv2, share2)

    def early(wave):
        pass

    start_ring(copy2, recv2)
    for h in range(2):
        inject(copy2, recv2, share2, h, prim[h])
    for step in range(1, HALFRING + 1):
        ring(copy1, recv1, step, lambda h, pp: inject(copy1, recv1, share1, h, pp))
        early(step)
        ring(copy2, recv2, step, lambda h, pp: inject(copy2, recv2, share2, h, pp))

    def bundle(h, step, j):
        if step in (0, HALFRING):
            ss = (sec[h] + step) % RING
            return [place(h, ss, near(h, 4 * j + n)) for n in range(4)]
        return [place(h, (sec[h] + way * step + RING) % RING, near(h, 2 * j + n))
                for n in range(2) for way in (-1, 1)]

    def unit(step, j):
        return j if step == 0 else 4 * step - 2 + j

    def held(h, slots, begin):
        return jnp.concatenate(
            [kvg[h, (yy * RING + zz) * 2 + c, begin:begin + 64, :] for yy, zz in slots], axis=0)

    half_lane = lax.broadcasted_iota(jnp.int32, (1, 128), 1) < 64

    def qk(step, j):
        for h in range(2):
            slots = bundle(h, step, j)
            u = unit(step, j)
            q = jnp.concatenate([qb[0, h], qb[1, h]], axis=0)
            s = lax.dot_general(
                q, held(h, slots, 0), (((1,), (1,)), ((), ())), preferred_element_type=F32)
            t = [tags[pl.ds((yy * RING + zz) * 2 + c, 1), :] for yy, zz in slots]
            for k in range(2):
                tops = [mx[h, 128 * k + 64 * g:128 * k + 64 * g + 64] for g in range(2)]
                for n in range(2):
                    tag = jnp.where(half_lane, t[2 * n], t[2 * n + 1])
                    seen = (tag == tok[k, 0]) | (tag == tok[k, 1])
                    for g in range(2):
                        r = 128 * k + 64 * g
                        part_s = jnp.where(seen, s[r:r + 64, 128 * n:128 * n + 128], NEG)
                        s3[h, u, r:r + 64, 128 * n:128 * n + 128] = part_s
                        tops[g] = jnp.maximum(tops[g], part_s)
                for g in range(2):
                    mx[h, 128 * k + 64 * g:128 * k + 64 * g + 64] = tops[g]

    def settle():
        for h in range(2):
            old = mrun[h]
            new = jnp.maximum(old, jnp.max(mx[h], axis=1, keepdims=True))
            factor = jnp.exp2((old - new) * scale2)
            mrun[h] = new
            acc[h] = acc[h] * jnp.concatenate([factor, factor], axis=1)

    ones = jnp.ones((256, HEAD), BF16)

    def pv(step, j, heads=(0, 1)):
        for h in heads:
            m = mrun[h]
            p = jnp.exp2((s3[h, unit(step, j)] - jnp.concatenate([m, m], axis=1)) * scale2)
            v = jnp.concatenate([held(h, bundle(h, step, j), 64), ones], axis=1)
            acc[h] += jnp.dot(p.astype(BF16), v, preferred_element_type=F32)

    def stage(relays, qk_step, pv_step, begin=0, end=HALFRING):
        def body(j, carry):
            for r in relays:
                for n in range(2):
                    relay(*r, 2 * j + n)
            if qk_step is not None:
                qk(qk_step, j)
            if pv_step is not None:
                pv(pv_step, j)
            return carry
        lax.fori_loop(begin, end, body, 0)

    trades[0].wait_recv()
    trades[1].wait_recv()
    stage([], 0, None, 0, 2)
    settle()
    stage([(*one, 1)], 1, 0, 0, 2)
    stage([(*one, 1)], 1, None, 2, 4)
    settle()
    stage([(*one, 2)], 2, 1)
    settle()
    stage([(*one, 3)], 3, 2)
    settle()
    stage([(*one, 4), (*two, 1)], None, 3)
    stage([], 4, None, 0, 2)
    settle()

    lane2 = lax.broadcasted_iota(jnp.int32, (128, 128), 1) < 64
    for h in range(2):
        def last(i, carry):
            pv(4, i, (h,))
            return carry
        lax.fori_loop(0, 2, last, 0)
        box[0, h, :, 0:HEAD] = acc[h, 128:256, 0:HEAD]
        box[0, h, :, HEAD:] = jnp.where(lane2, mrun[h, 128:256], acc[h, 128:256, HEAD:])
        trades[2 + h].start()
    stage([(*two, 2)], None, None)
    for h in range(2):
        trades[2 + h].wait_recv()
        m_here = mrun[h, 0:128]
        m_there = box[1, h, :, HEAD:HEAD + 1]
        top = jnp.maximum(m_here, m_there)
        w_here = jnp.exp2((m_here - top) * scale2)
        w_there = jnp.exp2((m_there - top) * scale2)
        mixed = acc[h, 0:128, 0:HEAD] * w_here + box[1, h, :, 0:HEAD] * w_there
        total = acc[h, 0:128, HEAD:] * w_here + box[1, h, :, 2 * HEAD - 1:2 * HEAD] * w_there
        a = (mixed / total).astype(BF16)
        for g in range(2):
            j = 2 * h + g
            attn_ref[:, j * HEAD:(j + 1) * HEAD] = a[g * 64:(g + 1) * 64]

    def arrived(all_of, sem):
        pltpu.make_async_remote_copy(
            src_ref=all_of, dst_ref=all_of, send_sem=send1.at[0], recv_sem=sem,
            device_id=mate, device_id_type=MESH).wait_recv()

    for h in range(2):
        arrived(kvg.at[h, 0:64, 128:ROWS], part1.at[h])

    def quarter(xx):
        return pl.ds(pl.multiple_of(xx * 512, 512), 512)

    def scatter(d):
        xx = (x + d) % 4
        return pltpu.make_async_remote_copy(
            src_ref=part.at[:, quarter(xx)], dst_ref=rsb.at[4 - d - 1], send_sem=xsend.at[0, d - 1],
            recv_sem=xrecv.at[0, 4 - d - 1], device_id=xdev(xx), device_id_type=MESH)

    for d in (2, 1, 3, 0):
        xx = (x + d) % 4
        w = [kvg[h, pl.ds(xx * 32, 32), 128 + 16 * g:144 + 16 * g, :].reshape(512, HEAD)
             for h in range(2) for g in range(2)]
        t = lax.dot_general(
            attn_ref[...], jnp.concatenate(w, axis=1), (((1,), (1,)), ((), ())),
            preferred_element_type=F32)
        part[:, quarter(xx)] = t.astype(BF16)
        if d > 0:
            scatter(d).start()

    stage([(*two, 3)], None, None)
    total = res_ref[:, quarter(x)].astype(F32) + part[:, quarter(x)].astype(F32)
    for d in range(1, 4):
        scatter(4 - d).wait_recv()
        total = total + rsb[d - 1].astype(F32)
    stream_ref[:, quarter(x)] = total.astype(BF16)

    def spread(d, xx):
        return pltpu.make_async_remote_copy(
            src_ref=stream_ref.at[:, quarter(xx)], dst_ref=stream_ref.at[:, quarter(xx)],
            send_sem=xsend.at[1, d - 1], recv_sem=xrecv.at[1, 4 - d - 1],
            device_id=xdev((x + d) % 4), device_id_type=MESH)

    for d in (2, 1, 3):
        spread(d, x).start()
    stage([(*two, 4)], None, None)
    for d in range(1, 4):
        spread(4 - d, (x + d) % 4).wait_recv()

    wide = stream_ref[...].astype(F32)
    mean = jnp.mean(wide * wide, axis=1, keepdims=True)
    normed[...] = (wide * lax.rsqrt(mean + 1e-06) * gain_ref[...]).astype(BF16)
    qacc[...] = jnp.zeros_like(qacc)
    for h in range(2):
        arrived(wqg.at[h, 0:64], part2.at[h])

    def qkv(yy, carry):
        n = normed[:, pl.ds(pl.multiple_of(yy * 256, 256), 256)]
        for h in range(2):
            qacc[:, h * 512:(h + 1) * 512] += jnp.dot(
                n, wqg[h, pl.ds(yy * 16, 16)].reshape(256, 512), preferred_element_type=F32)
        return carry

    lax.fori_loop(0, RING, qkv, 0)
    qkv_ref[...] = qacc[...].astype(BF16)

    for d in range(1, 4):
        scatter(d).wait_send()
        spread(d, x).wait_send()
    for t in trades:
        t.wait_send()

    def drain(sent, sem):
        pltpu.make_async_remote_copy(
            src_ref=sent, dst_ref=sent, send_sem=sem, recv_sem=recv1.at[0, 0, 0],
            device_id=mate, device_id_type=MESH).wait_send()

    for h in range(2):
        drain(kvg.at[h, 0:63], send1.at[h])
        drain(kvg.at[h, 0:64, 128:ROWS], sendm.at[h])
        drain(wqg.at[h, 0:63], send2.at[h])
        drain(wqg.at[h, 0:64], sendm.at[2 + h])


def hand_out(*refs):
    sources, results, sem = refs[0:3], refs[3:6], refs[6]
    outs = [pltpu.make_async_copy(sources[i], results[i], sem.at[i]) for i in range(3)]
    for copy in outs:
        copy.start()
    for copy in outs:
        copy.wait()


def on_device(
    fresh_queries, fresh_keys, fresh_values, cache, pool_root, branch_owner, branch_len,
    branch_root, request_branch, token_request, residual, wo_t, norm_gain, w_qkv,
):
    vmem = pl.BlockSpec(memory_space=pltpu.VMEM)
    args = (
        fresh_queries, fresh_keys, fresh_values, cache, pool_root.T, branch_owner.reshape(1, -1),
        branch_len.reshape(1, -1), branch_root.reshape(1, -1), request_branch, token_request,
        residual, wo_t, norm_gain.reshape(1, -1), w_qkv,
    )
    dma = pltpu.SemaphoreType.DMA
    shapes = tuple(jax.ShapeDtypeStruct((64, width), BF16) for width in (512, 2048, 1024))
    results = pl.pallas_call(
        kernel,
        out_shape=tuple(pltpu.VMEM(s.shape, BF16) for s in shapes),
        in_specs=[vmem] * len(args),
        out_specs=(vmem, vmem, vmem),
        scratch_shapes=[
            pltpu.VMEM((2, 2 * RING * RING, ROWS, HEAD), BF16),
            pltpu.VMEM((2, 2 * RING * RING, 16, 512), BF16),
            pltpu.VMEM((2, 2, 128, HEAD), BF16),
            pltpu.VMEM((2, 2, 64, 128), F32),
            pltpu.VMEM((2, 2 * RING, 256, 256), F32),
            pltpu.VMEM((2, 256, 128), F32),
            pltpu.VMEM((2, 256, 128), F32),
            pltpu.VMEM((2, 256, 256), F32),
            pltpu.VMEM((128, 128), F32),
            pltpu.VMEM((2, 2, 128, 256), F32),
            pltpu.VMEM((64, 2048), BF16),
            pltpu.VMEM((3, 64, 512), BF16),
            pltpu.VMEM((64, 2048), BF16),
            pltpu.VMEM((64, 1024), F32),
            dma((2,)),
            dma((2,)),
            dma((4,)),
            dma((2, RING, RING)),
            dma((2, RING, RING)),
            dma((2,)),
            dma((2,)),
            dma((2, 3)),
            dma((2, 3)),
            dma((2, 4)),
        ],
        compiler_params=pltpu.CompilerParams(
            collective_id=0, has_side_effects=True, vmem_limit_bytes=60 * 1024 * 1024),
    )(*args)
    return tuple(results)


def solution(mesh):
    return jax.shard_map(
        on_device,
        mesh=mesh,
        in_specs=(
            P("seq", "mp"),
            P("seq", "mp"),
            P("seq", "mp"),
            P(None, "seq", "mp"),
            P(),
            P(),
            P(),
            P(),
            P("seq", None),
            P("seq", None),
            P("seq", None),
            P("seq", "mp"),
            P(),
            P("seq", "mp"),
        ),
        out_specs=(P("seq", "mp"), P("seq", None), P("seq", "mp")),
        check_vma=False,
    )
```

```python
import math

import jax
import jax.numpy as jnp
from jax import lax
from jax.experimental import pallas as pl
from jax.experimental.pallas import tpu as pltpu
from jax.sharding import PartitionSpec as P

HEAD = 128
RING = 8
HALFRING = RING // 2
ROOTS = 32
ROWS = 160
NEG = -1e30
FLOOR = -1e9
MESH = pl.DeviceIdType.MESH
F32 = jnp.float32
BF16 = jnp.bfloat16


def kernel(
    q_ref, fk_ref, fv_ref, cache_ref, pool_ref, owner_ref, len_ref, broot_ref, rb_ref, tr_ref,
    res_ref, wo_ref, gain_ref, wq_ref,
    attn_ref, stream_ref, qkv_ref,
    kvg, wqg, qb, tok, s3, mx, mrun, acc, tags, box, part, rsb, normed, qacc,
    send1, send2, sendm, recv1, recv2, part1, part2, xsend, xrecv, swap,
):
    seq = lax.axis_index("seq")
    x = lax.axis_index("mp")
    y, z, c = seq // 16, (seq // 2) % RING, seq % 2
    scale2 = HEAD ** (-0.5) * math.log2(math.e)

    def dev(yy, zz, cc):
        return {"seq": (yy * RING + zz) * 2 + cc}

    def xdev(xx):
        return {"mp": xx}

    mate = dev(y, z, 1 - c)
    sec = (z, y)
    prim = (y, z)

    def place(h, ss, pp):
        return (pp, ss) if h == 0 else (ss, pp)

    def at(h, ss, pp):
        yy, zz = place(h, ss, pp)
        return dev(yy, zz, c)

    barrier = pltpu.get_barrier_semaphore()

    for d in (1, RING - 1):
        pl.semaphore_signal(barrier, inc=1, device_id=dev((y + d) % RING, z, c), device_id_type=MESH)
        pl.semaphore_signal(barrier, inc=1, device_id=dev(y, (z + d) % RING, c), device_id_type=MESH)
    pl.semaphore_signal(barrier, inc=1, device_id=mate, device_id_type=MESH)
    for d in range(1, 4):
        pl.semaphore_signal(barrier, inc=1, device_id=xdev((x + d) % 4), device_id_type=MESH)

    for h in range(2):
        kvg[h, seq, 0:64, :] = cache_ref[0, :, h * HEAD:(h + 1) * HEAD]
        kvg[h, seq, 64:128, :] = cache_ref[1, :, h * HEAD:(h + 1) * HEAD]
        for g in range(2):
            j = 2 * h + g
            kvg[h, seq, 128 + 16 * g:144 + 16 * g, :] = wo_ref[:, j * HEAD:(j + 1) * HEAD]

    pl.semaphore_wait(barrier, 4 + 1 + 3)

    def copy1(h, yy, zz, cc, sem, to):
        ref = kvg.at[h, (yy * RING + zz) * 2 + cc]
        return pltpu.make_async_remote_copy(
            src_ref=ref, dst_ref=ref, send_sem=send1.at[h], recv_sem=sem.at[h, yy, zz],
            device_id=to, device_id_type=MESH)

    def copy2(h, yy, zz, cc, sem, to):
        ref = wqg.at[h, (yy * RING + zz) * 2 + cc]
        return pltpu.make_async_remote_copy(
            src_ref=ref, dst_ref=ref, send_sem=send2.at[h], recv_sem=sem.at[h, yy, zz],
            device_id=to, device_id_type=MESH)

    def share1(h, yy, zz, cc):
        ref = kvg.at[h, (yy * RING + zz) * 2 + cc, 128:ROWS]
        return pltpu.make_async_remote_copy(
            src_ref=ref, dst_ref=ref, send_sem=sendm.at[h], recv_sem=part1.at[h],
            device_id=mate, device_id_type=MESH)

    def share2(h, yy, zz, cc):
        ref = wqg.at[h, (yy * RING + zz) * 2 + cc]
        return pltpu.make_async_remote_copy(
            src_ref=ref, dst_ref=ref, send_sem=sendm.at[2 + h], recv_sem=part2.at[h],
            device_id=mate, device_id_type=MESH)

    def trade(i, mine, theirs):
        return pltpu.make_async_remote_copy(
            src_ref=mine, dst_ref=theirs, send_sem=swap.at[0, i], recv_sem=swap.at[1, i],
            device_id=mate, device_id_type=MESH)

    trades = [trade(0, qb.at[0], qb.at[1]), trade(1, tok.at[0], tok.at[1]), trade(2, box.at[0, 0], box.at[1, 0]), trade(3, box.at[0, 1], box.at[1, 1])]

    def inject(copy, rsem, share, h, pp):
        yy, zz = place(h, sec[h], pp)
        copy(h, yy, zz, c, rsem, at(h, (sec[h] + 1) % RING, prim[h])).start()
        copy(h, yy, zz, c, rsem, at(h, (sec[h] + RING - 1) % RING, prim[h])).start()
        share(h, yy, zz, c).start()

    def start_ring(copy, rsem):
        for h in range(2):
            for way in (1, RING - 1):
                copy(h, y, z, c, rsem, at(h, sec[h], (prim[h] + way) % RING)).start()

    start_ring(copy1, recv1)
    for h in range(2):
        inject(copy1, recv1, share1, h, prim[h])

    for h in range(2):
        for g in range(2):
            j = 2 * h + g
            qb[0, h, g * 64:(g + 1) * 64, :] = q_ref[:, j * HEAD:(j + 1) * HEAD]
        wqg[h, seq] = wq_ref[:, h * 512:(h + 1) * 512]

    e_id = lax.broadcasted_iota(jnp.int32, (128, 128), 0)
    b_id = lax.broadcasted_iota(jnp.int32, (128, 128), 1)
    owns = owner_ref[...] == e_id
    owned = jnp.sum(jnp.where(owns, b_id.astype(F32), 0.0), axis=1, keepdims=True)
    olen = jnp.sum(jnp.where(owns, len_ref[...].astype(F32), 0.0), axis=1, keepdims=True)
    slot = lax.broadcasted_iota(jnp.int32, (128, 32), 1).astype(F32)
    btag = jnp.where(slot < olen, ROOTS + owned, -1.0)
    pool = pool_ref[...].astype(F32).T
    tags[...] = jnp.concatenate([pool, btag, pool, btag], axis=1)
    lane = lax.broadcasted_iota(jnp.int32, (64, 128), 1)

    tr = tr_ref[...].astype(F32)
    t_id = lax.broadcasted_iota(jnp.int32, (64, 64), 0)
    u_id = lax.broadcasted_iota(jnp.int32, (64, 64), 1)
    trc = jnp.sum(jnp.where(t_id == u_id, tr, 0.0), axis=1, keepdims=True)
    rb = rb_ref[...].astype(F32)
    tb = jnp.zeros((64, 1), F32)
    for r in range(4):
        tb = jnp.where(trc == float(r), rb[:, r:r + 1], tb)
    troot = jnp.sum(
        jnp.where(tb == lane.astype(F32), broot_ref[...].astype(F32), 0.0), axis=1, keepdims=True)
    tok[0, 0] = jnp.broadcast_to(troot, (64, 128))
    tok[0, 1] = jnp.broadcast_to(tb + ROOTS, (64, 128))
    trades[0].start()
    trades[1].start()


    own_seen = (tr == trc) & (u_id <= t_id)
    own_seen2 = jnp.concatenate([own_seen.astype(F32), own_seen.astype(F32)], axis=0) > 0.5
    ones64 = jnp.ones((64, HEAD), BF16)
    for h in range(2):
        s = lax.dot_general(
            qb[0, h], fk_ref[:, h * HEAD:(h + 1) * HEAD], (((1,), (1,)), ((), ())),
            preferred_element_type=F32)
        s = jnp.where(own_seen2, s, NEG)
        m = jnp.max(s, axis=1, keepdims=True)
        p = jnp.exp2((s - m) * scale2).astype(BF16)
        v = jnp.concatenate([fv_ref[:, h * HEAD:(h + 1) * HEAD], ones64], axis=1)
        acc[h, 0:128] = jnp.dot(p, v, preferred_element_type=F32)
        acc[h, 128:256] = jnp.zeros((128, 256), F32)
        mrun[h, 0:128] = jnp.broadcast_to(m, (128, 128))
        mrun[h, 128:256] = jnp.full((128, 128), FLOOR, F32)
        mx[h] = jnp.full((256, 128), NEG, F32)

    def wait_same(copy, rsem, h, yy, zz):
        copy(h, yy, zz, c, rsem, mate).wait_recv()

    def ring(copy, rsem, step, after):
        for h in range(2):
            ways = (1, -1) if step < HALFRING else (1,)
            for way in ways:
                pp = (prim[h] - way * step + RING) % RING
                yy, zz = place(h, sec[h], pp)
                wait_same(copy, rsem, h, yy, zz)
                last = step == HALFRING - 1
                if step < HALFRING - 1 or (last and way == (1 if h == 0 else -1)):
                    copy(h, yy, zz, c, rsem, at(h, sec[h], (prim[h] + way + RING) % RING)).start()
                if after is not None:
                    after(h, pp)

    def near(h, i):
        d = jnp.where(i % 2 == 1, (i + 1) // 2, RING - i // 2)
        return (prim[h] + d) % RING

    def relay(copy, rsem, share, step, i):
        for h in range(2):
            b = near(h, i)
            if step == HALFRING:
                yy, zz = place(h, (sec[h] + HALFRING) % RING, b)
                wait_same(copy, rsem, h, yy, zz)
                share(h, yy, zz, c).start()
                continue
            for way in (1, -1):
                yy, zz = place(h, (sec[h] - way * step + RING) % RING, b)
                wait_same(copy, rsem, h, yy, zz)
                onward = at(h, (sec[h] + way + RING) % RING, prim[h])
                if step < HALFRING - 1:
                    copy(h, yy, zz, c, rsem, onward).start()
                else:
                    @pl.when(i % 2 == (0 if way == 1 else 1))
                    def _():
                        copy(h, yy, zz, c, rsem, onward).start()
                share(h, yy, zz, c).start()

    one = (copy1, recv1, share1)
    two = (copy2, recv2, share2)

    def early(wave):
        if wave == 2:
            relay(*one, 1, 0)
            relay(*one, 1, 1)
        if wave == 3:
            relay(*one, 1, 2)
            relay(*one, 1, 3)
            relay(*one, 2, 0)
            relay(*one, 2, 1)

    start_ring(copy2, recv2)
    for h in range(2):
        inject(copy2, recv2, share2, h, prim[h])
    for step in range(1, HALFRING + 1):
        ring(copy1, recv1, step, lambda h, pp: inject(copy1, recv1, share1, h, pp))
        early(step)
        ring(copy2, recv2, step, lambda h, pp: inject(copy2, recv2, share2, h, pp))

    def bundle(h, step, j):
        if step in (0, HALFRING):
            ss = (sec[h] + step) % RING
            return [place(h, ss, near(h, 4 * j + n)) for n in range(4)]
        return [place(h, (sec[h] + way * step + RING) % RING, near(h, 2 * j + n))
                for n in range(2) for way in (-1, 1)]

    def unit(step, j):
        return j if step == 0 else 4 * step - 2 + j

    def held(h, slots, begin):
        return jnp.concatenate(
            [kvg[h, (yy * RING + zz) * 2 + c, begin:begin + 64, :] for yy, zz in slots], axis=0)

    half_lane = lax.broadcasted_iota(jnp.int32, (1, 128), 1) < 64

    def qk(step, j):
        for h in range(2):
            slots = bundle(h, step, j)
            u = unit(step, j)
            q = jnp.concatenate([qb[0, h], qb[1, h]], axis=0)
            s = lax.dot_general(
                q, held(h, slots, 0), (((1,), (1,)), ((), ())), preferred_element_type=F32)
            t = [tags[pl.ds((yy * RING + zz) * 2 + c, 1), :] for yy, zz in slots]
            for k in range(2):
                tops = [mx[h, 128 * k + 64 * g:128 * k + 64 * g + 64] for g in range(2)]
                for n in range(2):
                    tag = jnp.where(half_lane, t[2 * n], t[2 * n + 1])
                    seen = (tag == tok[k, 0]) | (tag == tok[k, 1])
                    for g in range(2):
                        r = 128 * k + 64 * g
                        part_s = jnp.where(seen, s[r:r + 64, 128 * n:128 * n + 128], NEG)
                        s3[h, u, r:r + 64, 128 * n:128 * n + 128] = part_s
                        tops[g] = jnp.maximum(tops[g], part_s)
                for g in range(2):
                    mx[h, 128 * k + 64 * g:128 * k + 64 * g + 64] = tops[g]

    def settle():
        for h in range(2):
            old = mrun[h]
            new = jnp.maximum(old, jnp.max(mx[h], axis=1, keepdims=True))
            factor = jnp.exp2((old - new) * scale2)
            mrun[h] = new
            acc[h] = acc[h] * jnp.concatenate([factor, factor], axis=1)

    ones = jnp.ones((256, HEAD), BF16)

    def pv(step, j, heads=(0, 1)):
        for h in heads:
            m = mrun[h]
            p = jnp.exp2((s3[h, unit(step, j)] - jnp.concatenate([m, m], axis=1)) * scale2)
            v = jnp.concatenate([held(h, bundle(h, step, j), 64), ones], axis=1)
            acc[h] += jnp.dot(p.astype(BF16), v, preferred_element_type=F32)

    def stage(relays, qk_step, pv_step, begin=0, end=HALFRING):
        def body(j, carry):
            for r in relays:
                for n in range(2):
                    relay(*r, 2 * j + n)
            if qk_step is not None:
                qk(qk_step, j)
            if pv_step is not None:
                pv(pv_step, j)
            return carry
        lax.fori_loop(begin, end, body, 0)

    trades[0].wait_recv()
    trades[1].wait_recv()
    stage([], 0, None, 0, 2)
    settle()
    stage([(*one, 1)], 1, None, 2, 4)
    stage([], 1, 0, 0, 2)
    settle()
    stage([(*one, 2)], 2, 1, 1, 4)
    stage([], 2, 1, 0, 1)
    settle()
    stage([(*one, 3)], 3, 2)
    settle()
    stage([(*one, 4), (*two, 1)], None, 3)
    stage([], 4, None, 0, 2)
    settle()

    lane2 = lax.broadcasted_iota(jnp.int32, (128, 128), 1) < 64
    for h in range(2):
        def last(i, carry):
            pv(4, i, (h,))
            return carry
        lax.fori_loop(0, 2, last, 0)
        box[0, h, :, 0:HEAD] = acc[h, 128:256, 0:HEAD]
        box[0, h, :, HEAD:] = jnp.where(lane2, mrun[h, 128:256], acc[h, 128:256, HEAD:])
        trades[2 + h].start()
    stage([(*two, 2)], None, None)
    for h in range(2):
        trades[2 + h].wait_recv()
        m_here = mrun[h, 0:128]
        m_there = box[1, h, :, HEAD:HEAD + 1]
        top = jnp.maximum(m_here, m_there)
        w_here = jnp.exp2((m_here - top) * scale2)
        w_there = jnp.exp2((m_there - top) * scale2)
        mixed = acc[h, 0:128, 0:HEAD] * w_here + box[1, h, :, 0:HEAD] * w_there
        total = acc[h, 0:128, HEAD:] * w_here + box[1, h, :, 2 * HEAD - 1:2 * HEAD] * w_there
        a = (mixed / total).astype(BF16)
        for g in range(2):
            j = 2 * h + g
            attn_ref[:, j * HEAD:(j + 1) * HEAD] = a[g * 64:(g + 1) * 64]

    def arrived(all_of, sem):
        pltpu.make_async_remote_copy(
            src_ref=all_of, dst_ref=all_of, send_sem=send1.at[0], recv_sem=sem,
            device_id=mate, device_id_type=MESH).wait_recv()

    for h in range(2):
        arrived(kvg.at[h, 0:64, 128:ROWS], part1.at[h])

    def quarter(xx):
        return pl.ds(pl.multiple_of(xx * 512, 512), 512)

    def scatter(d):
        xx = (x + d) % 4
        return pltpu.make_async_remote_copy(
            src_ref=part.at[:, quarter(xx)], dst_ref=rsb.at[4 - d - 1], send_sem=xsend.at[0, d - 1],
            recv_sem=xrecv.at[0, 4 - d - 1], device_id=xdev(xx), device_id_type=MESH)

    for d in (2, 1, 3, 0):
        xx = (x + d) % 4
        w = [kvg[h, pl.ds(xx * 32, 32), 128 + 16 * g:144 + 16 * g, :].reshape(512, HEAD)
             for h in range(2) for g in range(2)]
        t = lax.dot_general(
            attn_ref[...], jnp.concatenate(w, axis=1), (((1,), (1,)), ((), ())),
            preferred_element_type=F32)
        part[:, quarter(xx)] = t.astype(BF16)
        if d > 0:
            scatter(d).start()

    stage([(*two, 3)], None, None)
    total = res_ref[:, quarter(x)].astype(F32) + part[:, quarter(x)].astype(F32)
    for d in range(1, 4):
        scatter(4 - d).wait_recv()
        total = total + rsb[d - 1].astype(F32)
    stream_ref[:, quarter(x)] = total.astype(BF16)

    def spread(d, xx):
        return pltpu.make_async_remote_copy(
            src_ref=stream_ref.at[:, quarter(xx)], dst_ref=stream_ref.at[:, quarter(xx)],
            send_sem=xsend.at[1, d - 1], recv_sem=xrecv.at[1, 4 - d - 1],
            device_id=xdev((x + d) % 4), device_id_type=MESH)

    for d in (2, 1, 3):
        spread(d, x).start()
    stage([(*two, 4)], None, None)
    for d in range(1, 4):
        spread(4 - d, (x + d) % 4).wait_recv()

    wide = stream_ref[...].astype(F32)
    mean = jnp.mean(wide * wide, axis=1, keepdims=True)
    normed[...] = (wide * lax.rsqrt(mean + 1e-06) * gain_ref[...]).astype(BF16)
    qacc[...] = jnp.zeros_like(qacc)
    for h in range(2):
        arrived(wqg.at[h, 0:64], part2.at[h])

    def qkv(yy, carry):
        n = normed[:, quarter(yy)]
        for h in range(2):
            qacc[:, h * 512:(h + 1) * 512] += jnp.dot(
                n, wqg[h, pl.ds(yy * 32, 32)].reshape(512, 512), preferred_element_type=F32)
        return carry

    lax.fori_loop(0, 4, qkv, 0)
    qkv_ref[...] = qacc[...].astype(BF16)

    for d in range(1, 4):
        scatter(d).wait_send()
        spread(d, x).wait_send()
    for t in trades:
        t.wait_send()

    def drain(sent, sem):
        pltpu.make_async_remote_copy(
            src_ref=sent, dst_ref=sent, send_sem=sem, recv_sem=recv1.at[0, 0, 0],
            device_id=mate, device_id_type=MESH).wait_send()

    for h in range(2):
        drain(kvg.at[h, 0:63], send1.at[h])
        drain(kvg.at[h, 0:64, 128:ROWS], sendm.at[h])
        drain(wqg.at[h, 0:63], send2.at[h])
        drain(wqg.at[h, 0:64], sendm.at[2 + h])


def hand_out(*refs):
    sources, results, sem = refs[0:3], refs[3:6], refs[6]
    outs = [pltpu.make_async_copy(sources[i], results[i], sem.at[i]) for i in range(3)]
    for copy in outs:
        copy.start()
    for copy in outs:
        copy.wait()


def on_device(
    fresh_queries, fresh_keys, fresh_values, cache, pool_root, branch_owner, branch_len,
    branch_root, request_branch, token_request, residual, wo_t, norm_gain, w_qkv,
):
    vmem = pl.BlockSpec(memory_space=pltpu.VMEM)
    args = (
        fresh_queries, fresh_keys, fresh_values, cache, pool_root.T, branch_owner.reshape(1, -1),
        branch_len.reshape(1, -1), branch_root.reshape(1, -1), request_branch, token_request,
        residual, wo_t, norm_gain.reshape(1, -1), w_qkv,
    )
    dma = pltpu.SemaphoreType.DMA
    shapes = tuple(jax.ShapeDtypeStruct((64, width), BF16) for width in (512, 2048, 1024))
    results = pl.pallas_call(
        kernel,
        out_shape=tuple(pltpu.VMEM(s.shape, BF16) for s in shapes),
        in_specs=[vmem] * len(args),
        out_specs=(vmem, vmem, vmem),
        scratch_shapes=[
            pltpu.VMEM((2, 2 * RING * RING, ROWS, HEAD), BF16),
            pltpu.VMEM((2, 2 * RING * RING, 16, 512), BF16),
            pltpu.VMEM((2, 2, 128, HEAD), BF16),
            pltpu.VMEM((2, 2, 64, 128), F32),
            pltpu.VMEM((2, 2 * RING, 256, 256), F32),
            pltpu.VMEM((2, 256, 128), F32),
            pltpu.VMEM((2, 256, 128), F32),
            pltpu.VMEM((2, 256, 256), F32),
            pltpu.VMEM((128, 128), F32),
            pltpu.VMEM((2, 2, 128, 256), F32),
            pltpu.VMEM((64, 2048), BF16),
            pltpu.VMEM((3, 64, 512), BF16),
            pltpu.VMEM((64, 2048), BF16),
            pltpu.VMEM((64, 1024), F32),
            dma((2,)),
            dma((2,)),
            dma((4,)),
            dma((2, RING, RING)),
            dma((2, RING, RING)),
            dma((2,)),
            dma((2,)),
            dma((2, 3)),
            dma((2, 3)),
            dma((2, 4)),
        ],
        compiler_params=pltpu.CompilerParams(
            collective_id=0, has_side_effects=True, vmem_limit_bytes=60 * 1024 * 1024),
    )(*args)
    return tuple(results)


def solution(mesh):
    return jax.shard_map(
        on_device,
        mesh=mesh,
        in_specs=(
            P("seq", "mp"),
            P("seq", "mp"),
            P("seq", "mp"),
            P(None, "seq", "mp"),
            P(),
            P(),
            P(),
            P(),
            P("seq", None),
            P("seq", None),
            P("seq", None),
            P("seq", "mp"),
            P(),
            P("seq", "mp"),
        ),
        out_specs=(P("seq", "mp"), P("seq", None), P("seq", "mp")),
        check_vma=False,
    )
```

```python
import math

import jax
import jax.numpy as jnp
from jax import lax
from jax.experimental import pallas as pl
from jax.experimental.pallas import tpu as pltpu
from jax.sharding import PartitionSpec as P

HEAD = 128
RING = 8
HALFRING = RING // 2
ROOTS = 32
ROWS = 160
NEG = -1e30
FLOOR = -1e9
MESH = pl.DeviceIdType.MESH
F32 = jnp.float32
BF16 = jnp.bfloat16


def kernel(
    q_ref, fk_ref, fv_ref, cache_ref, pool_ref, owner_ref, len_ref, broot_ref, rb_ref, tr_ref,
    res_ref, wo_ref, gain_ref, wq_ref,
    attn_ref, stream_ref, qkv_ref,
    kvg, wqg, qb, tok, s3, mx, mrun, acc, tags, box, part, rsb, normed,
    send1, send2, sendm, recv1, recv2, part1, part2, xsend, xrecv, swap,
):
    seq = lax.axis_index("seq")
    x = lax.axis_index("mp")
    y, z, c = seq // 16, (seq // 2) % RING, seq % 2
    scale2 = HEAD ** (-0.5) * math.log2(math.e)

    def dev(yy, zz, cc):
        return {"seq": (yy * RING + zz) * 2 + cc}

    def xdev(xx):
        return {"mp": xx}

    mate = dev(y, z, 1 - c)
    sec = (z, y)
    prim = (y, z)

    def place(h, ss, pp):
        return (pp, ss) if h == 0 else (ss, pp)

    def at(h, ss, pp):
        yy, zz = place(h, ss, pp)
        return dev(yy, zz, c)

    barrier = pltpu.get_barrier_semaphore()

    for d in (1, RING - 1):
        pl.semaphore_signal(barrier, inc=1, device_id=dev((y + d) % RING, z, c), device_id_type=MESH)
        pl.semaphore_signal(barrier, inc=1, device_id=dev(y, (z + d) % RING, c), device_id_type=MESH)
    pl.semaphore_signal(barrier, inc=1, device_id=mate, device_id_type=MESH)
    for d in range(1, 4):
        pl.semaphore_signal(barrier, inc=1, device_id=xdev((x + d) % 4), device_id_type=MESH)

    for h in range(2):
        kvg[h, seq, 0:64, :] = cache_ref[0, :, h * HEAD:(h + 1) * HEAD]
        kvg[h, seq, 64:128, :] = cache_ref[1, :, h * HEAD:(h + 1) * HEAD]
        for g in range(2):
            j = 2 * h + g
            kvg[h, seq, 128 + 16 * g:144 + 16 * g, :] = wo_ref[:, j * HEAD:(j + 1) * HEAD]

    pl.semaphore_wait(barrier, 4 + 1 + 3)

    def copy1(h, yy, zz, cc, sem, to):
        ref = kvg.at[h, (yy * RING + zz) * 2 + cc]
        return pltpu.make_async_remote_copy(
            src_ref=ref, dst_ref=ref, send_sem=send1.at[h], recv_sem=sem.at[h, yy, zz],
            device_id=to, device_id_type=MESH)

    def copy2(h, yy, zz, cc, sem, to):
        ref = wqg.at[h, (yy * RING + zz) * 2 + cc]
        return pltpu.make_async_remote_copy(
            src_ref=ref, dst_ref=ref, send_sem=send2.at[h], recv_sem=sem.at[h, yy, zz],
            device_id=to, device_id_type=MESH)

    def share1(h, yy, zz, cc):
        ref = kvg.at[h, (yy * RING + zz) * 2 + cc, 128:ROWS]
        return pltpu.make_async_remote_copy(
            src_ref=ref, dst_ref=ref, send_sem=sendm.at[h], recv_sem=part1.at[h],
            device_id=mate, device_id_type=MESH)

    def share2(h, yy, zz, cc):
        ref = wqg.at[h, (yy * RING + zz) * 2 + cc]
        return pltpu.make_async_remote_copy(
            src_ref=ref, dst_ref=ref, send_sem=sendm.at[2 + h], recv_sem=part2.at[h],
            device_id=mate, device_id_type=MESH)

    def trade(i, mine, theirs):
        return pltpu.make_async_remote_copy(
            src_ref=mine, dst_ref=theirs, send_sem=swap.at[0, i], recv_sem=swap.at[1, i],
            device_id=mate, device_id_type=MESH)

    trades = [trade(0, qb.at[0], qb.at[1]), trade(1, tok.at[0], tok.at[1]), trade(2, box.at[0, 0], box.at[1, 0]), trade(3, box.at[0, 1], box.at[1, 1])]

    def inject(copy, rsem, share, h, pp):
        yy, zz = place(h, sec[h], pp)
        copy(h, yy, zz, c, rsem, at(h, (sec[h] + 1) % RING, prim[h])).start()
        copy(h, yy, zz, c, rsem, at(h, (sec[h] + RING - 1) % RING, prim[h])).start()
        share(h, yy, zz, c).start()

    def start_ring(copy, rsem):
        for h in range(2):
            for way in (1, RING - 1):
                copy(h, y, z, c, rsem, at(h, sec[h], (prim[h] + way) % RING)).start()

    start_ring(copy1, recv1)
    for h in range(2):
        inject(copy1, recv1, share1, h, prim[h])

    for h in range(2):
        for g in range(2):
            j = 2 * h + g
            qb[0, h, g * 64:(g + 1) * 64, :] = q_ref[:, j * HEAD:(j + 1) * HEAD]
        wqg[h, seq] = wq_ref[:, h * 512:(h + 1) * 512]

    e_id = lax.broadcasted_iota(jnp.int32, (128, 128), 0)
    b_id = lax.broadcasted_iota(jnp.int32, (128, 128), 1)
    owns = owner_ref[...] == e_id
    owned = jnp.sum(jnp.where(owns, b_id.astype(F32), 0.0), axis=1, keepdims=True)
    olen = jnp.sum(jnp.where(owns, len_ref[...].astype(F32), 0.0), axis=1, keepdims=True)
    slot = lax.broadcasted_iota(jnp.int32, (128, 32), 1).astype(F32)
    btag = jnp.where(slot < olen, ROOTS + owned, -1.0)
    pool = pool_ref[...].astype(F32).T
    tags[...] = jnp.concatenate([pool, btag, pool, btag], axis=1)
    lane = lax.broadcasted_iota(jnp.int32, (64, 128), 1)

    tr = tr_ref[...].astype(F32)
    t_id = lax.broadcasted_iota(jnp.int32, (64, 64), 0)
    u_id = lax.broadcasted_iota(jnp.int32, (64, 64), 1)
    trc = jnp.sum(jnp.where(t_id == u_id, tr, 0.0), axis=1, keepdims=True)
    rb = rb_ref[...].astype(F32)
    tb = jnp.zeros((64, 1), F32)
    for r in range(4):
        tb = jnp.where(trc == float(r), rb[:, r:r + 1], tb)
    troot = jnp.sum(
        jnp.where(tb == lane.astype(F32), broot_ref[...].astype(F32), 0.0), axis=1, keepdims=True)
    tok[0, 0] = jnp.broadcast_to(troot, (64, 128))
    tok[0, 1] = jnp.broadcast_to(tb + ROOTS, (64, 128))
    trades[0].start()
    trades[1].start()


    own_seen = (tr == trc) & (u_id <= t_id)
    own_seen2 = jnp.concatenate([own_seen.astype(F32), own_seen.astype(F32)], axis=0) > 0.5
    ones64 = jnp.ones((64, HEAD), BF16)
    for h in range(2):
        s = lax.dot_general(
            qb[0, h], fk_ref[:, h * HEAD:(h + 1) * HEAD], (((1,), (1,)), ((), ())),
            preferred_element_type=F32)
        s = jnp.where(own_seen2, s, NEG)
        m = jnp.max(s, axis=1, keepdims=True)
        p = jnp.exp2((s - m) * scale2).astype(BF16)
        v = jnp.concatenate([fv_ref[:, h * HEAD:(h + 1) * HEAD], ones64], axis=1)
        acc[h, 0:128] = jnp.dot(p, v, preferred_element_type=F32)
        acc[h, 128:256] = jnp.zeros((128, 256), F32)
        mrun[h, 0:128] = jnp.broadcast_to(m, (128, 128))
        mrun[h, 128:256] = jnp.full((128, 128), FLOOR, F32)
        mx[h] = jnp.full((256, 128), NEG, F32)

    def wait_same(copy, rsem, h, yy, zz):
        copy(h, yy, zz, c, rsem, mate).wait_recv()

    def ring(copy, rsem, step, after):
        for h in range(2):
            ways = (1, -1) if step < HALFRING else (1,)
            for way in ways:
                pp = (prim[h] - way * step + RING) % RING
                yy, zz = place(h, sec[h], pp)
                wait_same(copy, rsem, h, yy, zz)
                last = step == HALFRING - 1
                if step < HALFRING - 1 or (last and way == (1 if h == 0 else -1)):
                    copy(h, yy, zz, c, rsem, at(h, sec[h], (prim[h] + way + RING) % RING)).start()
                if after is not None:
                    after(h, pp)

    def near(h, i):
        d = jnp.where(i % 2 == 1, (i + 1) // 2, RING - i // 2)
        return (prim[h] + d) % RING

    def relay(copy, rsem, share, step, i):
        for h in range(2):
            b = near(h, i)
            if step == HALFRING:
                yy, zz = place(h, (sec[h] + HALFRING) % RING, b)
                wait_same(copy, rsem, h, yy, zz)
                share(h, yy, zz, c).start()
                continue
            for way in (1, -1):
                yy, zz = place(h, (sec[h] - way * step + RING) % RING, b)
                wait_same(copy, rsem, h, yy, zz)
                onward = at(h, (sec[h] + way + RING) % RING, prim[h])
                if step < HALFRING - 1:
                    copy(h, yy, zz, c, rsem, onward).start()
                else:
                    @pl.when(i % 2 == (0 if way == 1 else 1))
                    def _():
                        copy(h, yy, zz, c, rsem, onward).start()
                share(h, yy, zz, c).start()

    one = (copy1, recv1, share1)
    two = (copy2, recv2, share2)

    def early(wave):
        if wave == 2:
            relay(*one, 1, 0)
            relay(*one, 1, 1)
        if wave == 3:
            relay(*one, 1, 2)
            relay(*one, 1, 3)
            relay(*one, 2, 0)
            relay(*one, 2, 1)

    start_ring(copy2, recv2)
    for h in range(2):
        inject(copy2, recv2, share2, h, prim[h])
    for step in range(1, HALFRING + 1):
        ring(copy1, recv1, step, lambda h, pp: inject(copy1, recv1, share1, h, pp))
        early(step)
        ring(copy2, recv2, step, lambda h, pp: inject(copy2, recv2, share2, h, pp))

    def bundle(h, step, j):
        if step in (0, HALFRING):
            ss = (sec[h] + step) % RING
            return [place(h, ss, near(h, 4 * j + n)) for n in range(4)]
        return [place(h, (sec[h] + way * step + RING) % RING, near(h, 2 * j + n))
                for n in range(2) for way in (-1, 1)]

    def unit(step, j):
        return j if step == 0 else 4 * step - 2 + j

    def held(h, slots, begin):
        return jnp.concatenate(
            [kvg[h, (yy * RING + zz) * 2 + c, begin:begin + 64, :] for yy, zz in slots], axis=0)

    half_lane = lax.broadcasted_iota(jnp.int32, (1, 128), 1) < 64

    def qk(step, j):
        for h in range(2):
            slots = bundle(h, step, j)
            u = unit(step, j)
            q = jnp.concatenate([qb[0, h], qb[1, h]], axis=0)
            s = lax.dot_general(
                q, held(h, slots, 0), (((1,), (1,)), ((), ())), preferred_element_type=F32)
            t = [tags[pl.ds((yy * RING + zz) * 2 + c, 1), :] for yy, zz in slots]
            for k in range(2):
                tops = [mx[h, 128 * k + 64 * g:128 * k + 64 * g + 64] for g in range(2)]
                for n in range(2):
                    tag = jnp.where(half_lane, t[2 * n], t[2 * n + 1])
                    seen = (tag == tok[k, 0]) | (tag == tok[k, 1])
                    for g in range(2):
                        r = 128 * k + 64 * g
                        part_s = jnp.where(seen, s[r:r + 64, 128 * n:128 * n + 128], NEG)
                        s3[h, u, r:r + 64, 128 * n:128 * n + 128] = part_s
                        tops[g] = jnp.maximum(tops[g], part_s)
                for g in range(2):
                    mx[h, 128 * k + 64 * g:128 * k + 64 * g + 64] = tops[g]

    def settle():
        for h in range(2):
            old = mrun[h]
            new = jnp.maximum(old, jnp.max(mx[h], axis=1, keepdims=True))
            factor = jnp.exp2((old - new) * scale2)
            mrun[h] = new
            acc[h] = acc[h] * jnp.concatenate([factor, factor], axis=1)

    ones = jnp.ones((256, HEAD), BF16)

    def pv(step, j, heads=(0, 1)):
        for h in heads:
            m = mrun[h]
            p = jnp.exp2((s3[h, unit(step, j)] - jnp.concatenate([m, m], axis=1)) * scale2)
            v = jnp.concatenate([held(h, bundle(h, step, j), 64), ones], axis=1)
            acc[h] += jnp.dot(p.astype(BF16), v, preferred_element_type=F32)

    def stage(relays, qk_step, pv_step, begin=0, end=HALFRING):
        def body(j, carry):
            for r in relays:
                for n in range(2):
                    relay(*r, 2 * j + n)
            if qk_step is not None:
                qk(qk_step, j)
            if pv_step is not None:
                pv(pv_step, j)
            return carry
        lax.fori_loop(begin, end, body, 0)

    trades[0].wait_recv()
    trades[1].wait_recv()
    stage([], 0, None, 0, 2)
    settle()
    stage([(*one, 1)], 1, None, 2, 4)
    stage([], 1, 0, 0, 2)
    settle()
    stage([(*one, 2)], 2, 1, 1, 4)
    stage([], 2, 1, 0, 1)
    settle()
    stage([(*one, 3)], 3, 2)
    settle()
    stage([(*one, 4), (*two, 1)], None, 3)
    stage([], 4, None, 0, 2)
    settle()

    lane2 = lax.broadcasted_iota(jnp.int32, (128, 128), 1) < 64
    for h in range(2):
        def last(i, carry):
            pv(4, i, (h,))
            return carry
        lax.fori_loop(0, 2, last, 0)
        box[0, h, :, 0:HEAD] = acc[h, 128:256, 0:HEAD]
        box[0, h, :, HEAD:] = jnp.where(lane2, mrun[h, 128:256], acc[h, 128:256, HEAD:])
        trades[2 + h].start()
    stage([(*two, 2)], None, None)
    for h in range(2):
        trades[2 + h].wait_recv()
        m_here = mrun[h, 0:128]
        m_there = box[1, h, :, HEAD:HEAD + 1]
        top = jnp.maximum(m_here, m_there)
        w_here = jnp.exp2((m_here - top) * scale2)
        w_there = jnp.exp2((m_there - top) * scale2)
        mixed = acc[h, 0:128, 0:HEAD] * w_here + box[1, h, :, 0:HEAD] * w_there
        total = acc[h, 0:128, HEAD:] * w_here + box[1, h, :, 2 * HEAD - 1:2 * HEAD] * w_there
        a = (mixed / total).astype(BF16)
        for g in range(2):
            j = 2 * h + g
            attn_ref[:, j * HEAD:(j + 1) * HEAD] = a[g * 64:(g + 1) * 64]

    def arrived(all_of, sem):
        pltpu.make_async_remote_copy(
            src_ref=all_of, dst_ref=all_of, send_sem=send1.at[0], recv_sem=sem,
            device_id=mate, device_id_type=MESH).wait_recv()

    for h in range(2):
        arrived(kvg.at[h, 0:64, 128:ROWS], part1.at[h])

    def quarter(xx):
        return pl.ds(pl.multiple_of(xx * 512, 512), 512)

    def scatter(d):
        xx = (x + d) % 4
        return pltpu.make_async_remote_copy(
            src_ref=part.at[:, quarter(xx)], dst_ref=rsb.at[4 - d - 1], send_sem=xsend.at[0, d - 1],
            recv_sem=xrecv.at[0, 4 - d - 1], device_id=xdev(xx), device_id_type=MESH)

    for d in (2, 1, 3, 0):
        xx = (x + d) % 4
        w = [kvg[h, pl.ds(xx * 32, 32), 128 + 16 * g:144 + 16 * g, :].reshape(512, HEAD)
             for h in range(2) for g in range(2)]
        t = lax.dot_general(
            attn_ref[...], jnp.concatenate(w, axis=1), (((1,), (1,)), ((), ())),
            preferred_element_type=F32)
        part[:, quarter(xx)] = t.astype(BF16)
        if d > 0:
            scatter(d).start()

    stage([(*two, 3)], None, None)
    total = res_ref[:, quarter(x)].astype(F32) + part[:, quarter(x)].astype(F32)
    for d in range(1, 4):
        scatter(4 - d).wait_recv()
        total = total + rsb[d - 1].astype(F32)
    stream_ref[:, quarter(x)] = total.astype(BF16)

    def spread(d, xx):
        return pltpu.make_async_remote_copy(
            src_ref=stream_ref.at[:, quarter(xx)], dst_ref=stream_ref.at[:, quarter(xx)],
            send_sem=xsend.at[1, d - 1], recv_sem=xrecv.at[1, 4 - d - 1],
            device_id=xdev((x + d) % 4), device_id_type=MESH)

    for d in (2, 1, 3):
        spread(d, x).start()
    stage([(*two, 4)], None, None)
    for d in range(1, 4):
        spread(4 - d, (x + d) % 4).wait_recv()

    wide = stream_ref[...].astype(F32)
    mean = jnp.mean(wide * wide, axis=1, keepdims=True)
    normed[...] = (wide * lax.rsqrt(mean + 1e-06) * gain_ref[...]).astype(BF16)
    for h in range(2):
        arrived(wqg.at[h, 0:64], part2.at[h])

    for h in range(2):
        sums = jnp.zeros((64, 512), F32)
        for yy in range(4):
            sums = sums + jnp.dot(
                normed[:, yy * 512:(yy + 1) * 512], wqg[h, yy * 32:(yy + 1) * 32].reshape(512, 512),
                preferred_element_type=F32)
        qkv_ref[:, h * 512:(h + 1) * 512] = sums.astype(BF16)

    for d in range(1, 4):
        scatter(d).wait_send()
        spread(d, x).wait_send()
    for t in trades:
        t.wait_send()

    def drain(sent, sem):
        pltpu.make_async_remote_copy(
            src_ref=sent, dst_ref=sent, send_sem=sem, recv_sem=recv1.at[0, 0, 0],
            device_id=mate, device_id_type=MESH).wait_send()

    for h in range(2):
        drain(kvg.at[h, 0:63], send1.at[h])
        drain(kvg.at[h, 0:64, 128:ROWS], sendm.at[h])
        drain(wqg.at[h, 0:63], send2.at[h])
        drain(wqg.at[h, 0:64], sendm.at[2 + h])


def hand_out(*refs):
    sources, results, sem = refs[0:3], refs[3:6], refs[6]
    outs = [pltpu.make_async_copy(sources[i], results[i], sem.at[i]) for i in range(3)]
    for copy in outs:
        copy.start()
    for copy in outs:
        copy.wait()


def on_device(
    fresh_queries, fresh_keys, fresh_values, cache, pool_root, branch_owner, branch_len,
    branch_root, request_branch, token_request, residual, wo_t, norm_gain, w_qkv,
):
    vmem = pl.BlockSpec(memory_space=pltpu.VMEM)
    args = (
        fresh_queries, fresh_keys, fresh_values, cache, pool_root.T, branch_owner.reshape(1, -1),
        branch_len.reshape(1, -1), branch_root.reshape(1, -1), request_branch, token_request,
        residual, wo_t, norm_gain.reshape(1, -1), w_qkv,
    )
    dma = pltpu.SemaphoreType.DMA
    shapes = tuple(jax.ShapeDtypeStruct((64, width), BF16) for width in (512, 2048, 1024))
    results = pl.pallas_call(
        kernel,
        out_shape=tuple(pltpu.VMEM(s.shape, BF16) for s in shapes),
        in_specs=[vmem] * len(args),
        out_specs=(vmem, vmem, vmem),
        scratch_shapes=[
            pltpu.VMEM((2, 2 * RING * RING, ROWS, HEAD), BF16),
            pltpu.VMEM((2, 2 * RING * RING, 16, 512), BF16),
            pltpu.VMEM((2, 2, 128, HEAD), BF16),
            pltpu.VMEM((2, 2, 64, 128), F32),
            pltpu.VMEM((2, 2 * RING, 256, 256), F32),
            pltpu.VMEM((2, 256, 128), F32),
            pltpu.VMEM((2, 256, 128), F32),
            pltpu.VMEM((2, 256, 256), F32),
            pltpu.VMEM((128, 128), F32),
            pltpu.VMEM((2, 2, 128, 256), F32),
            pltpu.VMEM((64, 2048), BF16),
            pltpu.VMEM((3, 64, 512), BF16),
            pltpu.VMEM((64, 2048), BF16),
            dma((2,)),
            dma((2,)),
            dma((4,)),
            dma((2, RING, RING)),
            dma((2, RING, RING)),
            dma((2,)),
            dma((2,)),
            dma((2, 3)),
            dma((2, 3)),
            dma((2, 4)),
        ],
        compiler_params=pltpu.CompilerParams(
            collective_id=0, has_side_effects=True, vmem_limit_bytes=60 * 1024 * 1024),
    )(*args)
    return tuple(results)


def solution(mesh):
    return jax.shard_map(
        on_device,
        mesh=mesh,
        in_specs=(
            P("seq", "mp"),
            P("seq", "mp"),
            P("seq", "mp"),
            P(None, "seq", "mp"),
            P(),
            P(),
            P(),
            P(),
            P("seq", None),
            P("seq", None),
            P("seq", None),
            P("seq", "mp"),
            P(),
            P("seq", "mp"),
        ),
        out_specs=(P("seq", "mp"), P("seq", None), P("seq", "mp")),
        check_vma=False,
    )
```
